128 devices in a mesh: row: 16 (over y_hi, x, core), col: 8 (over y_lo, z).
Axes of the slice: x: 4, y: 4 (y_hi: 2, y_lo: 2; y = y_hi * 2 + y_lo), z: 4, core: 2. Of those that a mesh axis runs over, the one named last changes fastest.
Arguments:
- pair_feature_map: bfloat16 [64, 1024, 1024], P(None, 'row', 'col'), may hold values from -6 to 6
- conv_weight: bfloat16 [3, 3, 64, 64], replicated, may hold values from -0.25 to 0.25
- conv_bias: float32 [64], replicated, may hold values from -3 to 3
- cotangent: bfloat16 [64, 1024, 1024], P(None, 'row', 'col'), may hold values from -6 to 6
Outputs:
- symmetric: bfloat16 [64, 1024, 1024], P(None, 'row', 'col')
- grad_input: bfloat16 [64, 1024, 1024], P(None, 'row', 'col')
- grad_weight: float32 [3, 3, 64, 64], replicated
- grad_bias: float32 [64], replicated
The draws below stay inside these ranges and needn't reach their ends.
All inputs are finite; a program needn't handle non-finite values.
Results may differ from the reference program's by a relative error of at most 0.0085.
Values may be sent and summed in bfloat16 or wider, within the bound.
A program may use at most 128 MiB of HBM per device.

```python
import jax
import jax.numpy as jnp
from jax import lax

C = 64
DILATION_STEP = 8
L = 1024


def steps_of(stream_key, extent, cuts, low, high):
    factor_of, own = 1.0, jax.random.fold_in(stream_key, 6)
    for dim, blocks in cuts:
        draws = jnp.exp(jax.random.uniform(jax.random.fold_in(own, dim), (blocks,), jnp.float32, low / len(cuts), high / len(cuts)))
        factor_of = factor_of * jnp.repeat(draws, extent[dim] // blocks).reshape([-1 if axis == dim else 1 for axis in range(len(extent))])
    return factor_of


def centred(rng, shape, spread, limit, split=(), dtype=jnp.bfloat16):
    values = jax.random.normal(rng, shape, jnp.float32) * spread
    if len(split) > 0:
        values = steps_of(rng, shape, split, -0.22, 0.18) * values
    return jnp.clip(values, min=-limit, max=limit).astype(dtype)


def setup_inputs(seed: int = 0) -> dict:
    streams_of = jax.random.split(jax.random.key(seed), 5)
    return {
        "pair_feature_map": centred(streams_of[0], (C, L, L), 1.0, 6.0, ((1, 16), (2, 8))),
        "conv_weight": centred(streams_of[1], (3, 3, C, C), (9 * C) ** -0.5, 0.25),
        "conv_bias": centred(streams_of[2], (C,), 0.5, 3.0, (), jnp.float32),
        "cotangent": centred(streams_of[3], (C, L, L), 1.0, 6.0, ((1, 16), (2, 8))),
    }


def tap_block(padded_input, conv_weight, leading_row, block_row_span, flip):
    channel_count = padded_input.shape[0]
    map_width = padded_input.shape[2] - 2 * DILATION_STEP
    anchor_point = jnp.zeros((), jnp.int32)
    total = jnp.zeros((channel_count, block_row_span, map_width), jnp.float32)
    for row_kernel_tap in range(3):
        for column_tap in range(3):
            row_offset = 2 - row_kernel_tap if flip else row_kernel_tap
            column_offset = 2 - column_tap if flip else column_tap
            block_portion = lax.dynamic_slice(padded_input, (anchor_point, leading_row + DILATION_STEP * row_offset, anchor_point + DILATION_STEP * column_offset), (channel_count, block_row_span, map_width)).astype(jnp.float32)
            matrix = conv_weight[row_kernel_tap, column_tap].astype(jnp.float32)
            if flip:
                matrix = matrix.T
            total = total + jnp.einsum("oi,ihw->ohw", matrix, block_portion)
    return total


def weight_block(gradient_padded, pair_feature_map, leading_row, block_row_span):
    channel_count = pair_feature_map.shape[0]
    map_width = pair_feature_map.shape[2]
    anchor_point = jnp.zeros((), jnp.int32)
    rows_x = lax.dynamic_slice(pair_feature_map, (anchor_point, leading_row, anchor_point), (channel_count, block_row_span, map_width)).astype(jnp.float32)
    grads = []
    for row_kernel_tap in range(3):
        for column_tap in range(3):
            block_portion = lax.dynamic_slice(gradient_padded, (anchor_point, leading_row + DILATION_STEP * (2 - row_kernel_tap), anchor_point + DILATION_STEP * (2 - column_tap)), (channel_count, block_row_span, map_width)).astype(jnp.float32)
            grads.append(jnp.einsum("ohw,ihw->oi", block_portion, rows_x))
    return jnp.stack(grads).reshape(3, 3, channel_count, channel_count)


def join_blocks(stacked):
    return jnp.transpose(stacked, (1, 0, 2, 3)).reshape(stacked.shape[1], -1, stacked.shape[3])


def reference(pair_feature_map, conv_weight, conv_bias, cotangent):
    block_count = 8
    block_row_span = L // block_count
    starts = (jnp.arange(block_count) * block_row_span).astype(jnp.int32)
    border_edges = ((0, 0), (DILATION_STEP, DILATION_STEP), (DILATION_STEP, DILATION_STEP))
    padded_input = jnp.pad(pair_feature_map, border_edges)
    pre_blocks = lax.map(lambda leading_row: tap_block(padded_input, conv_weight, leading_row, block_row_span, False), starts)
    pre_act = join_blocks(pre_blocks) + conv_bias[:, None, None]
    mixed_map = (pair_feature_map.astype(jnp.float32) + jax.nn.elu(pre_act)).astype(jnp.bfloat16)
    symmetric = (mixed_map.astype(jnp.float32) + jnp.transpose(mixed_map, (0, 2, 1)).astype(jnp.float32)).astype(jnp.bfloat16)
    grad_mixed = cotangent.astype(jnp.float32) + jnp.transpose(cotangent, (0, 2, 1)).astype(jnp.float32)
    elu_slope = jnp.where(pre_act > 0, jnp.float32(1.0), jnp.exp(jnp.minimum(pre_act, jnp.float32(0.0))))
    gradient_preactivation = (grad_mixed * elu_slope).astype(jnp.bfloat16)
    gradient_padded = jnp.pad(gradient_preactivation, border_edges)

    def backward(leading_row):
        back = tap_block(gradient_padded, conv_weight, leading_row, block_row_span, True)
        return back, weight_block(gradient_padded, pair_feature_map, leading_row, block_row_span)

    back_blocks, weight_parts = lax.map(backward, starts)
    grad_input = (grad_mixed + join_blocks(back_blocks)).astype(jnp.bfloat16)
    grad_weight = jnp.sum(weight_parts, axis=0) / L
    grad_bias = jnp.sum(gradient_preactivation.astype(jnp.float32), axis=(1, 2)) / L
    return symmetric, grad_input, grad_weight, grad_bias
```

```python
import functools

import jax
import jax.numpy as jnp
from jax import lax
from jax.experimental import pallas as pl
from jax.experimental.pallas import tpu as pltpu
from jax.sharding import PartitionSpec as P

MESH = pl.DeviceIdType.MESH
F32 = jnp.float32
BF16 = jnp.bfloat16

C = 64
R = 64
W = 128
D = 8
PIECES = 32


def position():
    r, c = lax.axis_index("row"), lax.axis_index("col")
    return r, c


def swap_middle(y):
    return jnp.where(jnp.logical_or(y == 1, y == 2), 3 - y, y)


def swap_outer(y):
    return jnp.where(jnp.logical_or(y == 0, y == 3), 3 - y, y)


def next_stop(stage, p):
    r, c = position()
    x, core, z = (r // 2) % 4, r % 2, c % 4
    y = 2 * (r // 8) + c // 4
    first_axis, j, how = p % 2, (p // 2) % 4, p // 8
    u = jnp.where(first_axis == 0, x, z)
    v = jnp.where(first_axis == 0, z, x)
    if stage == 0:
        u = (u + v + j) % 4
    elif stage == 1:
        v = (u - j - v + 8) % 4
    else:
        u = (u - v - j + 8) % 4
    nx = jnp.where(first_axis == 0, u, v)
    nz = jnp.where(first_axis == 0, v, u)
    around = swap_outer(y) if stage == 1 else y + 1 - 2 * (y % 2)
    ny = jnp.where(how == 3, around, jnp.where(how == stage, swap_middle(y), y))
    nr = (ny // 2) * 8 + nx * 2 + core
    nc = (ny % 2) * 4 + nz
    return nr, nc, jnp.logical_and(nr == r, nc == c)


def relay_copy(stops, s, p, ssem, rsem):
    nr, nc, here = next_stop(s, p)
    remote = pltpu.make_async_remote_copy(
        stops[s].at[p], stops[s + 1].at[p], ssem.at[s, p], rsem.at[s, p],
        device_id=(nr, nc), device_id_type=MESH)
    local = pltpu.make_async_copy(stops[s].at[p], stops[s + 1].at[p], rsem.at[s, p])
    return remote, local, here


def relay_start(stops, s, p, ssem, rsem):
    remote, local, here = relay_copy(stops, s, p, ssem, rsem)

    @pl.when(here)
    def _():
        local.start()

    @pl.when(jnp.logical_not(here))
    def _():
        remote.start()


def relay_arrived(stops, s, p, ssem, rsem):
    _, local, _ = relay_copy(stops, s, p, ssem, rsem)
    local.wait()


def relay_sent(stops, s, p, ssem, rsem):
    remote, _, here = relay_copy(stops, s, p, ssem, rsem)

    @pl.when(jnp.logical_not(here))
    def _():
        remote.wait_send()


def loop(n, body):
    def step(i, carry):
        body(i)
        return carry

    lax.fori_loop(0, n, step, 0)


def lanes(shape):
    return lax.broadcasted_iota(jnp.int32, shape, 1)


def rows_halo(stack, ssem, rsem):
    r, c = position()
    up = pltpu.make_async_remote_copy(
        stack.at[1, pl.ds(R, D)], stack.at[1, pl.ds(0, D)], ssem.at[0], rsem.at[0],
        device_id=(jnp.minimum(r + 1, 15), c), device_id_type=MESH)
    down = pltpu.make_async_remote_copy(
        stack.at[1, pl.ds(D, D)], stack.at[1, pl.ds(R + D, D)], ssem.at[1], rsem.at[1],
        device_id=(jnp.maximum(r - 1, 0), c), device_id_type=MESH)
    return up, down, r < 15, r > 0


def cols_halo(packed, edges, ssem, rsem):
    r, c = position()
    right = pltpu.make_async_remote_copy(
        packed.at[1], edges.at[0], ssem.at[2], rsem.at[2],
        device_id=(r, jnp.minimum(c + 1, 7)), device_id_type=MESH)
    left = pltpu.make_async_remote_copy(
        packed.at[0], edges.at[1], ssem.at[3], rsem.at[3],
        device_id=(r, jnp.maximum(c - 1, 0)), device_id_type=MESH)
    return right, left, c < 7, c > 0


def halo_start(copies):
    fore, back, has_next, has_previous = copies

    @pl.when(has_next)
    def _():
        fore.start()

    @pl.when(has_previous)
    def _():
        back.start()


def halo_arrived(copies):
    fore, back, has_next, has_previous = copies

    @pl.when(has_previous)
    def _():
        fore.wait_recv()

    @pl.when(has_next)
    def _():
        back.wait_recv()


def halo_sent(copies):
    fore, back, has_next, has_previous = copies

    @pl.when(has_next)
    def _():
        fore.wait_send()

    @pl.when(has_previous)
    def _():
        back.wait_send()


def clear_edges(stack, edges):
    r, c = position()
    zero_rows = jnp.zeros((D, C, W), BF16)
    zero_cols = jnp.zeros(edges.shape[1:], BF16)

    @pl.when(r == 0)
    def _():
        stack[1, 0:D] = zero_rows

    @pl.when(r == 15)
    def _():
        stack[1, R + D : R + 2 * D] = zero_rows

    @pl.when(c == 0)
    def _():
        edges[0] = zero_cols

    @pl.when(c == 7)
    def _():
        edges[1] = zero_cols


def pack_columns(stack, packed):
    lane = lanes((C, W))

    def group(g):
        first = jnp.zeros((C, W), F32)
        last = jnp.zeros((C, W), F32)
        for k in range(16):
            v = stack[1, 16 * g + k].astype(F32)
            mine = jnp.logical_and(lane >= 8 * k, lane < 8 * k + 8)
            first = jnp.where(mine, pltpu.roll(v, 8 * k, 1) if k else v, first)
            last = jnp.where(mine, pltpu.roll(v, (8 * k + 8) % W, 1) if k < 15 else v, last)
        packed[0, g] = first.astype(BF16)
        packed[1, g] = last.astype(BF16)

    loop(5, group)


def shift_columns(stack, edges):
    lane = lanes((C, W))

    def group(g):
        before = edges[0, g].astype(F32)
        after = edges[1, g].astype(F32)
        for k in range(16):
            v = stack[1, 16 * g + k].astype(F32)
            b = pltpu.roll(before, (W - 8 * k) % W, 1) if k else before
            a = pltpu.roll(after, (W - 8 - 8 * k) % W, 1) if k < 15 else after
            stack[0, 16 * g + k] = jnp.where(lane < D, b, pltpu.roll(v, D, 1)).astype(BF16)
            stack[2, 16 * g + k] = jnp.where(lane >= W - D, a, pltpu.roll(v, W - D, 1)).astype(BF16)

    loop(5, group)


def pair_rows(stack, r):
    parts = []
    for p in range(3):
        for q in range(3):
            parts.append(jnp.concatenate([stack[q, r + D * p], stack[q, r + 1 + D * p]], axis=1))
    return jnp.concatenate(parts, axis=0)


def split_halves(source, kept, sent):
    r, _ = position()
    core = r % 2
    lane = lanes((R, W))

    def pair(i):
        a = source[i].astype(F32)
        b = source[i + PIECES].astype(F32)
        low = jnp.where(lane < 64, a, pltpu.roll(b, 64, 1)).astype(BF16)
        high = jnp.where(lane < 64, pltpu.roll(a, 64, 1), b).astype(BF16)
        is_low = core == 0
        kept[i, core] = jnp.where(is_low, low, high)
        sent[i] = jnp.where(is_low, high, low)

    loop(PIECES, pair)


def core_exchange(sent, kept, ssem, rsem):
    r, c = position()
    core = r % 2
    return pltpu.make_async_remote_copy(
        sent, kept.at[:, core], ssem, rsem,
        device_id=(r + 1 - 2 * core, c), device_id_type=MESH)


def flip_pair(kept, stop, i):
    block = kept[i].reshape(2 * R, W)
    stop[i] = jnp.transpose(block.astype(F32), (1, 0)).astype(BF16).reshape(2, R, W)


def kernel(x_ref, cot_ref, wf_ref, wb_ref, bias_ref, sym_ref, gin_ref, gw_ref, gb_ref,
           flat, xs, gs, slope, mixed, xpack, xedge, gpack, gedge,
           csend, ckeep, c0, c1, c2, c3, msend, mkeep, m0, m1, m2, m3,
           gsum, rs_in, rs_mine, ar_in, ag,
           core_ssem, core_rsem, xh_ssem, xh_rsem, gh_ssem, gh_rsem,
           c_ssem, c_rsem, m_ssem, m_rsem, rs_ssem, rs_rsem, ar_ssem, ar_rsem, ag_ssem, ag_rsem):
    r, c = position()
    barrier = pltpu.get_barrier_semaphore()
    loop(128, lambda i: pl.semaphore_signal(barrier, 1, device_id=(i // 8, i % 8), device_id_type=MESH))

    cstops, mstops = (c0, c1, c2, c3), (m0, m1, m2, m3)
    cot_there = core_exchange(csend, ckeep, core_ssem.at[0], core_rsem.at[0])
    cot_here = pltpu.make_async_remote_copy(
        csend, ckeep.at[:, 1 - r % 2], core_ssem.at[0], core_rsem.at[0],
        device_id=(r + 1 - 2 * (r % 2), c), device_id_type=MESH)
    mix_there = core_exchange(msend, mkeep, core_ssem.at[1], core_rsem.at[1])
    mix_here = pltpu.make_async_remote_copy(
        msend, mkeep.at[:, 1 - r % 2], core_ssem.at[1], core_rsem.at[1],
        device_id=(r + 1 - 2 * (r % 2), c), device_id_type=MESH)

    split_halves(cot_ref, ckeep, csend)
    clear_edges(xs, xedge)
    clear_edges(gs, gedge)
    pl.semaphore_wait(barrier, 128)
    cot_there.start()

    def widen(i):
        flat[pl.ds(pl.multiple_of(i * R, R), R), :] = x_ref[i].astype(F32)

    loop(C, widen)

    def to_row(i):
        xs[1, i + D] = flat[pl.ds(i, C, stride=R), :].astype(BF16)

    loop(R, to_row)
    xrows = rows_halo(xs, xh_ssem, xh_rsem)
    halo_start(xrows)

    cot_here.wait_recv()

    def cot_out(i):
        flip_pair(ckeep, c0, i)
        relay_start(cstops, 0, i, c_ssem, c_rsem)

    loop(PIECES, cot_out)

    halo_arrived(xrows)
    pack_columns(xs, xpack)
    xcols = cols_halo(xpack, xedge, xh_ssem, xh_rsem)
    halo_start(xcols)
    halo_arrived(xcols)
    shift_columns(xs, xedge)

    bias2 = jnp.concatenate([bias_ref[...], bias_ref[...]], axis=1)

    def forward(i):
        row = 2 * i
        pre = jnp.dot(wf_ref[...], pair_rows(xs, row), preferred_element_type=F32) + bias2
        e = jnp.exp(jnp.minimum(pre, 0.0))
        up = pre > 0
        act = jnp.where(up, pre, e - 1.0)
        slp = jnp.where(up, 1.0, e)
        for k in range(2):
            at = slice(k * W, (k + 1) * W)
            value = xs[1, row + k + D].astype(F32) + act[:, at]
            flat[pl.ds(row + k, C, stride=R), :] = value
            slope[row + k] = slp[:, at]

    loop(R // 4, forward)

    def pass_on(stops, s, ssem, rsem):
        def one(i):
            relay_arrived(stops, s, i, ssem, rsem)
            relay_start(stops, s + 1, i, ssem, rsem)

        loop(PIECES, one)

    pass_on(cstops, 0, c_ssem, c_rsem)
    loop(R // 4, lambda i: forward(i + R // 4))

    def narrow(i):
        mixed[i] = flat[pl.ds(pl.multiple_of(i * R, R), R), :].astype(BF16)

    loop(C, narrow)
    split_halves(mixed, mkeep, msend)
    mix_there.start()
    pass_on(cstops, 1, c_ssem, c_rsem)
    mix_here.wait_recv()

    def mix_out(i):
        flip_pair(mkeep, m0, i)
        relay_start(mstops, 0, i, m_ssem, m_rsem)

    loop(PIECES, mix_out)

    def grad_mixed(i):
        relay_arrived(cstops, 2, i, c_ssem, c_rsem)
        for h in range(2):
            ch = i + PIECES * h
            flat[pl.ds(pl.multiple_of(ch * R, R), R), :] = (
                cot_ref[ch].astype(F32) + c3[i, h].astype(F32))

    loop(PIECES, grad_mixed)

    def grad_pre(i):
        gs[1, i + D] = (flat[pl.ds(i, C, stride=R), :] * slope[i]).astype(BF16)

    loop(R, grad_pre)
    grows = rows_halo(gs, gh_ssem, gh_rsem)
    halo_start(grows)

    gsum[...] = jnp.zeros(gsum.shape, F32)

    def weight_step(i):
        row = 2 * i
        g = jnp.concatenate([gs[1, row + D], gs[1, row + 1 + D]], axis=1)
        gsum[:, 0 : 9 * C] += lax.dot_general(
            g, pair_rows(xs, row), (((1,), (1,)), ((), ())), preferred_element_type=F32)
        g32 = g.astype(F32)
        gsum[:, 640:768] += g32[:, 0:W] + g32[:, W : 2 * W]

    loop(R // 2, weight_step)
    gsum[:, 640:768] = jnp.broadcast_to(jnp.sum(gsum[:, 640:768], axis=1, keepdims=True), (C, W))

    def own_piece(k):
        og, half = k // 2, k % 2
        return gsum.at[pl.ds(pl.multiple_of(og * 8, 8), 8), pl.ds(pl.multiple_of(half * 384, 384), 384)]

    def rs_copy(k):
        return pltpu.make_async_remote_copy(
            own_piece(k), rs_in.at[r], rs_ssem.at[k], rs_rsem.at[r], device_id=(k, c), device_id_type=MESH)

    def rs_wait(k):
        return pltpu.make_async_remote_copy(
            own_piece(k), rs_in.at[k], rs_ssem.at[k], rs_rsem.at[k], device_id=(k, c), device_id_type=MESH)

    def others(n, me, body):
        def one(k):
            @pl.when(k != me)
            def _():
                body(k)

        loop(n, one)

    others(16, r, lambda k: rs_copy(k).start())
    pass_on(mstops, 0, m_ssem, m_rsem)
    halo_arrived(grows)
    pack_columns(gs, gpack)
    gcols = cols_halo(gpack, gedge, gh_ssem, gh_rsem)
    halo_start(gcols)

    rs_in[r] = own_piece(r)[...]
    others(16, r, lambda k: rs_wait(k).wait_recv())
    rs_mine[...] = jnp.sum(rs_in[...], axis=0)

    def ar_copy(k, slot):
        return pltpu.make_async_remote_copy(
            rs_mine, ar_in.at[slot], ar_ssem.at[k], ar_rsem.at[slot], device_id=(r, k), device_id_type=MESH)

    others(8, c, lambda k: ar_copy(k, c).start())
    halo_arrived(gcols)
    shift_columns(gs, gedge)
    pass_on(mstops, 1, m_ssem, m_rsem)
    ar_in[c] = rs_mine[...]
    others(8, c, lambda k: ar_copy(k, k).wait_recv())
    ag[r] = jnp.sum(ar_in[...], axis=0) * (1.0 / 1024)

    def ag_copy(k, slot):
        return pltpu.make_async_remote_copy(
            ag.at[r], ag.at[slot], ag_ssem.at[k], ag_rsem.at[slot], device_id=(k, c), device_id_type=MESH)

    others(16, r, lambda k: ag_copy(k, r).start())

    def backward(i):
        row = 2 * i
        back = jnp.dot(wb_ref[...], pair_rows(gs, row), preferred_element_type=F32)
        for k in range(2):
            flat[pl.ds(row + k, C, stride=R), :] = back[:, k * W : (k + 1) * W]

    loop(R // 2, backward)

    def input_out(i):
        for h in range(2):
            ch = i + PIECES * h
            gm = cot_ref[ch].astype(F32) + c3[i, h].astype(F32)
            gin_ref[ch] = (gm + flat[pl.ds(pl.multiple_of(ch * R, R), R), :]).astype(BF16)

    loop(PIECES, input_out)

    def sym_out(i):
        relay_arrived(mstops, 2, i, m_ssem, m_rsem)
        for h in range(2):
            ch = i + PIECES * h
            sym_ref[ch] = (mixed[ch].astype(F32) + m3[i, h].astype(F32)).astype(BF16)

    loop(PIECES, sym_out)

    others(16, r, lambda k: ag_copy(k, k).wait_recv())
    for og in range(8):
        gw_ref[og * 8 : og * 8 + 8, 0:384] = ag[2 * og]
        gw_ref[og * 8 : og * 8 + 8, 384:768] = ag[2 * og + 1]
    gb_ref[...] = jnp.zeros(gb_ref.shape, F32)

    cot_there.wait_send()
    mix_there.wait_send()
    for copies in (xrows, xcols, grows, gcols):
        halo_sent(copies)
    for s in range(3):
        loop(PIECES, lambda i: relay_sent(cstops, s, i, c_ssem, c_rsem))
        loop(PIECES, lambda i: relay_sent(mstops, s, i, m_ssem, m_rsem))
    others(16, r, lambda k: rs_copy(k).wait_send())
    others(8, c, lambda k: ar_copy(k, c).wait_send())
    others(16, r, lambda k: ag_copy(k, r).wait_send())


def block(x, weight, bias, cot):
    wf = jnp.transpose(weight, (2, 0, 1, 3)).reshape(C, 9 * C)
    wb = jnp.transpose(weight[::-1, ::-1], (3, 0, 1, 2)).reshape(C, 9 * C)
    bias_full = jnp.broadcast_to(bias[:, None], (C, W))
    vmem = pl.BlockSpec(memory_space=pltpu.VMEM)
    tile = pltpu.VMEM((C, R, W), BF16)
    stop = pltpu.VMEM((PIECES, 2, R, W), BF16)
    stack = pltpu.VMEM((3, R + 2 * D, C, W), BF16)
    columns = pltpu.VMEM((2, 5, C, W), BF16)
    dma = pltpu.SemaphoreType.DMA
    sym, gin, gw, _ = pl.pallas_call(
        kernel,
        out_shape=(
            jax.ShapeDtypeStruct((C, R, W), BF16),
            jax.ShapeDtypeStruct((C, R, W), BF16),
            jax.ShapeDtypeStruct((C, 768), F32),
            jax.ShapeDtypeStruct((8, W), F32),
        ),
        in_specs=[vmem] * 5,
        out_specs=[vmem] * 4,
        scratch_shapes=[
            pltpu.VMEM((C * R, W), F32), stack, stack, pltpu.VMEM((R, C, W), F32), tile,
            columns, columns, columns, columns,
            pltpu.VMEM((PIECES, R, W), BF16), stop, stop, stop, stop, stop,
            pltpu.VMEM((PIECES, R, W), BF16), stop, stop, stop, stop, stop,
            pltpu.VMEM((C, 768), F32), pltpu.VMEM((16, 8, 384), F32), pltpu.VMEM((8, 384), F32),
            pltpu.VMEM((8, 8, 384), F32), pltpu.VMEM((16, 8, 384), F32),
            dma((2,)), dma((2,)), dma((4,)), dma((4,)), dma((4,)), dma((4,)),
            dma((3, PIECES)), dma((3, PIECES)), dma((3, PIECES)), dma((3, PIECES)),
            dma((16,)), dma((16,)), dma((8,)), dma((8,)), dma((16,)), dma((16,)),
        ],
        compiler_params=pltpu.CompilerParams(
            collective_id=0, has_side_effects=True, vmem_limit_bytes=60 * 1024 * 1024),
    )(x, cot, wf, wb, bias_full)
    grad_weight = jnp.transpose(gw[:, : 9 * C].reshape(C, 3, 3, C), (1, 2, 0, 3))
    return sym, gin, grad_weight, gw[:, 640]


def solution(mesh):
    tile = P(None, "row", "col")
    return jax.shard_map(
        block,
        mesh=mesh,
        in_specs=(tile, P(), P(), tile),
        out_specs=(tile, tile, P(), P()),
        check_vma=False,
    )
```

```python
import functools

import jax
import jax.numpy as jnp
from jax import lax
from jax.experimental import pallas as pl
from jax.experimental.pallas import tpu as pltpu
from jax.sharding import PartitionSpec as P

MESH = pl.DeviceIdType.MESH
F32 = jnp.float32
BF16 = jnp.bfloat16

C = 64
R = 64
W = 128
D = 8
PIECES = 32


def position():
    return lax.axis_index("row"), lax.axis_index("col")


def mod4(n):
    return lax.rem(n, 4)


def swap_middle(y):
    return jnp.where(jnp.logical_or(y == 1, y == 2), 3 - y, y)


def swap_outer(y):
    return jnp.where(jnp.logical_or(y == 0, y == 3), 3 - y, y)


def next_stop(stage, p):
    mode, n = p
    r, c = position()
    chip_row, core = lax.div(r, 2), lax.rem(r, 2)
    x, z = mod4(chip_row), mod4(c)
    y = 2 * lax.div(chip_row, 4) + lax.div(c, 4)
    j, how = mod4(n), lax.div(n, 4)
    u, v = (z, x) if mode else (x, z)
    if stage == 0:
        u = mod4(u + v + j)
    elif stage == 1:
        v = mod4(u - j - v + 8)
    else:
        u = mod4(u - v - j + 8)
    nx, nz = (v, u) if mode else (u, v)
    around = swap_outer(y) if stage == 1 else y + 1 - 2 * lax.rem(y, 2)
    ny = jnp.where(how == 3, around, jnp.where(how == stage, swap_middle(y), y))
    nr = lax.div(ny, 2) * 8 + nx * 2 + core
    nc = lax.rem(ny, 2) * 4 + nz
    return nr, nc, jnp.logical_and(nr == r, nc == c)


def relay_copy(stops, s, p, sems):
    nr, nc, here = next_stop(s, p)
    mode, n = p
    i = 2 * n + mode
    ssem, rsem = sems
    remote = lambda: pltpu.make_async_remote_copy(
        stops[s].at[i], stops[s + 1].at[i], ssem.at[s, i], rsem.at[s, i],
        device_id=(nr, nc), device_id_type=MESH)
    local = lambda: pltpu.make_async_copy(stops[s].at[i], stops[s + 1].at[i], rsem.at[s, i])
    return remote, local, here


def relay_start(stops, s, p, sems):
    remote, local, here = relay_copy(stops, s, p, sems)

    @pl.when(here)
    def _():
        local().start()

    @pl.when(jnp.logical_not(here))
    def _():
        remote().start()


def relay_arrived(stops, s, p, sems):
    i = 2 * p[1] + p[0]
    pltpu.make_async_copy(stops[s].at[i], stops[s + 1].at[i], sems[1].at[s, i]).wait()


def relay_sent(stops, s, p, sems):
    remote, _, here = relay_copy(stops, s, p, sems)

    @pl.when(jnp.logical_not(here))
    def _():
        remote().wait_send()


def pass_on(stops, s, n, sems):
    for mode in range(2):
        relay_arrived(stops, s, (mode, n), sems)
        relay_start(stops, s + 1, (mode, n), sems)


def loop(n, body):
    def step(i, carry):
        body(i)
        return carry

    lax.fori_loop(0, n, step, 0)


def lanes(shape):
    return lax.broadcasted_iota(jnp.int32, shape, 1)


class Halo:
    def __init__(self, stack, packed, edges, ssem, rsem):
        self.stack, self.edges, self.packed = stack, edges, packed
        self.sems = ssem, rsem
        r, c = position()
        up, down, left, right = r > 0, r < 15, c > 0, c < 7
        both = jnp.logical_and
        self.moves = [
            (stack.at[1, pl.ds(R + D, D)], stack.at[1, pl.ds(D, D)], 1, 0, down, up),
            (stack.at[1, pl.ds(2 * D, D)], stack.at[1, pl.ds(R + 2 * D, D)], -1, 0, up, down),
            (packed.at[1], edges.at[0, pl.ds(1, 4)], 0, 1, right, left),
            (packed.at[0], edges.at[1, pl.ds(1, 4)], 0, -1, left, right),
            (packed.at[1, 3], edges.at[0, 0], 1, 1, both(down, right), both(up, left)),
            (packed.at[0, 3], edges.at[1, 0], 1, -1, both(down, left), both(up, right)),
            (packed.at[1, 0], edges.at[0, 5], -1, 1, both(up, right), both(down, left)),
            (packed.at[0, 0], edges.at[1, 5], -1, -1, both(up, left), both(down, right)),
        ]

    def copy(self, k):
        r, c = position()
        source, target, dr, dc, _, _ = self.moves[k]
        ssem, rsem = self.sems
        return pltpu.make_async_remote_copy(
            source, target, ssem.at[k], rsem.at[k],
            device_id=(jnp.clip(r + dr, 0, 15), jnp.clip(c + dc, 0, 7)), device_id_type=MESH)

    def start(self):
        for k in range(8):
            pl.when(self.moves[k][4])(lambda: self.copy(k).start())

    def arrived(self):
        for k in range(8):
            pl.when(self.moves[k][5])(lambda: self.copy(k).wait_recv())

    def sent(self):
        for k in range(8):
            pl.when(self.moves[k][4])(lambda: self.copy(k).wait_send())

    def clear(self):
        stack, edges = self.stack, self.edges
        r, c = position()
        zero_rows = jnp.zeros((D, C, W), BF16)
        zero_corner = jnp.zeros((C, W), BF16)
        zero_cols = jnp.zeros(edges.shape[1:], BF16)

        @pl.when(r == 0)
        def _():
            stack[1, D : 2 * D] = zero_rows
            edges[0, 0] = zero_corner
            edges[1, 0] = zero_corner

        @pl.when(r == 15)
        def _():
            stack[1, R + 2 * D : R + 3 * D] = zero_rows
            edges[0, 5] = zero_corner
            edges[1, 5] = zero_corner

        @pl.when(c == 0)
        def _():
            edges[0] = zero_cols

        @pl.when(c == 7)
        def _():
            edges[1] = zero_cols

    def pack(self):
        stack, packed = self.stack, self.packed
        lane = lanes((C, W))

        def group(g):
            first = jnp.zeros((C, W), F32)
            last = jnp.zeros((C, W), F32)
            for k in range(16):
                v = stack[1, 16 * g + k + 16].astype(F32)
                mine = jnp.logical_and(lane >= 8 * k, lane < 8 * k + 8)
                first = jnp.where(mine, pltpu.roll(v, 8 * k, 1) if k else v, first)
                last = jnp.where(mine, pltpu.roll(v, (8 * k + 8) % W, 1) if k < 15 else v, last)
            packed[0, g] = first.astype(BF16)
            packed[1, g] = last.astype(BF16)

        loop(4, group)

    def shift(self):
        stack, edges = self.stack, self.edges
        lane = lanes((C, W))

        def eight(g, half):
            before = edges[0, g].astype(F32)
            after = edges[1, g].astype(F32)
            for k in range(8 * half, 8 * half + 8):
                v = stack[1, 16 * g + k].astype(F32)
                b = pltpu.roll(before, (W - 8 * k) % W, 1) if k else before
                a = pltpu.roll(after, (W - 8 - 8 * k) % W, 1) if k < 15 else after
                stack[0, 16 * g + k] = jnp.where(lane < D, b, pltpu.roll(v, D, 1)).astype(BF16)
                stack[2, 16 * g + k] = jnp.where(lane >= W - D, a, pltpu.roll(v, W - D, 1)).astype(BF16)

        def group(i):
            eight(i, 1)
            eight(i + 1, 0)

        loop(5, group)


def tap_rows(stack, row, count):
    parts = []
    for p in range(3):
        for q in range(3):
            parts.append(jnp.concatenate([stack[q, row + D + D * p + k] for k in range(count)], axis=1))
    return jnp.concatenate(parts, axis=0)


def split_pair(a, b, i, kept, sent):
    core = lax.rem(position()[0], 2)
    lane = lanes((R, W))
    low = jnp.where(lane < 64, a, pltpu.roll(b, 64, 1)).astype(BF16)
    high = jnp.where(lane < 64, pltpu.roll(a, 64, 1), b).astype(BF16)
    is_low = core == 0
    kept[i, core] = jnp.where(is_low, low, high)
    sent[i] = jnp.where(is_low, high, low)


class CoreExchange:
    def __init__(self, sent, kept, ssem, rsem):
        self.refs = sent, kept, ssem, rsem

    def copy(self, k, core):
        sent, kept, ssem, rsem = self.refs
        r, c = position()
        part = pl.ds(8 * k, 8)
        return pltpu.make_async_remote_copy(
            sent.at[part], kept.at[part, core], ssem.at[k], rsem.at[k],
            device_id=(r + 1 - 2 * lax.rem(r, 2), c), device_id_type=MESH)

    def start(self, k):
        self.copy(k, lax.rem(position()[0], 2)).start()

    def arrived(self, k):
        self.copy(k, 1 - lax.rem(position()[0], 2)).wait_recv()

    def sent(self):
        loop(4, lambda k: self.copy(k, lax.rem(position()[0], 2)).wait_send())


def flip_out(exchange, kept, stops, sems):
    def part(k):
        exchange.arrived(k)

        def two(n):
            for mode in range(2):
                i = 2 * n + mode
                block = kept[i].reshape(2 * R, W)
                stops[0][i] = jnp.transpose(block, (1, 0)).reshape(2, R, W)
                relay_start(stops, 0, (mode, n), sems)

        loop(4, lambda m: two(4 * k + m))

    loop(4, part)


def others(n, me, body):
    def one(k):
        @pl.when(k != me)
        def _():
            body(k)

    loop(n, one)


def kernel(x_ref, cot_ref, w_ref, bias_ref, sym_ref, gin_ref, gw_ref, gb_ref,
           x_in, cot_in, wf, wb, bias2, flat, xs, gs, gzero, slope, mixed, xpack, xedge, gpack, gedge,
           csend, ckeep, c0, c1, c2, c3, msend, mkeep, m0, m1, m2, m3,
           gsum, gall, rs_in, rs_mine, ar_in, ag,
           in_sem, cc_ssem, cc_rsem, mc_ssem, mc_rsem, xh_ssem, xh_rsem, gh_ssem, gh_rsem,
           c_ssem, c_rsem, m_ssem, m_rsem, rs_ssem, rs_rsem, ar_ssem, ar_rsem, ag_ssem, ag_rsem):
    r, c = position()
    barrier = pltpu.get_barrier_semaphore()
    loop(128, lambda i: pl.semaphore_signal(
        barrier, 1, device_id=(lax.div(i, 8), lax.rem(i, 8)), device_id_type=MESH))
    x_copy = pltpu.make_async_copy(x_ref, x_in, in_sem.at[0])
    cot_copy = pltpu.make_async_copy(cot_ref, cot_in, in_sem.at[1])
    cot_copy.start()
    x_copy.start()

    cstops, mstops = (c0, c1, c2, c3), (m0, m1, m2, m3)
    csems, msems = (c_ssem, c_rsem), (m_ssem, m_rsem)
    cot_cores = CoreExchange(csend, ckeep, cc_ssem, cc_rsem)
    mix_cores = CoreExchange(msend, mkeep, mc_ssem, mc_rsem)
    xhalo = Halo(xs, xpack, xedge, xh_ssem, xh_rsem)
    ghalo = Halo(gs, gpack, gedge, gh_ssem, gh_rsem)

    spot = lax.broadcasted_iota(jnp.int32, (C, W), 0)
    left = (spot == lanes((C, W))).astype(BF16)
    right = (spot + C == lanes((C, W))).astype(BF16)
    for t in range(0, 9, 2):
        for out, at, dims in ((wf, lambda t: (t // 3, t % 3), ((1,), (0,))),
                              (wb, lambda t: (2 - t // 3, 2 - t % 3), ((0,), (0,)))):
            value = lax.dot_general(w_ref[at(t)], left, (dims, ((), ())), preferred_element_type=F32)
            if t < 8:
                value += lax.dot_general(w_ref[at(t + 1)], right, (dims, ((), ())), preferred_element_type=F32)
            out[:, C * t : C * t + W] = value.astype(BF16)
    bias2[...] = jnp.transpose(jnp.broadcast_to(bias_ref[...], (W, C)), (1, 0))

    xhalo.clear()
    ghalo.clear()
    gzero[0:16] = jnp.zeros((16, C, W), BF16)
    gzero[80:96] = jnp.zeros((16, C, W), BF16)
    cot_copy.wait()
    loop(PIECES, lambda i: split_pair(cot_in[i].astype(F32), cot_in[i + PIECES].astype(F32), i, ckeep, csend))
    x_copy.wait()

    def widen(i):
        flat[pl.ds(pl.multiple_of(i * R, R), R), :] = x_in[i].astype(F32)

    loop(C, widen)

    def to_row(i):
        xs[1, i + 16] = flat[pl.ds(i, C, stride=R), :].astype(BF16)

    loop(R, to_row)
    xhalo.pack()
    pl.semaphore_wait(barrier, 128)
    loop(4, cot_cores.start)
    xhalo.start()
    flip_out(cot_cores, ckeep, cstops, csems)
    xhalo.arrived()
    xhalo.shift()
    wide_bias = jnp.concatenate([bias2[...]] * 4, axis=1)

    def forward(i):
        row = 4 * i
        pre = jnp.dot(wf[:, 0 : 9 * C], tap_rows(xs, row, 4), preferred_element_type=F32) + wide_bias
        e = jnp.exp(jnp.minimum(pre, 0.0))
        up = pre > 0
        act = jnp.where(up, pre, e - 1.0)
        slp = jnp.where(up, 1.0, e)
        for k in range(4):
            at = slice(k * W, (k + 1) * W)
            value = xs[1, row + k + 16].astype(F32) + act[:, at]
            flat[pl.ds(row + k, C, stride=R), :] = value
            slope[row + k] = slp[:, at]
        pass_on(cstops, 0, i, csems)

    loop(R // 4, forward)

    def split_mixed(n):
        for mode in range(2):
            i = 2 * n + mode
            a = flat[pl.ds(pl.multiple_of(i * R, R), R), :]
            b = flat[pl.ds(pl.multiple_of((i + PIECES) * R, R), R), :]
            mixed[i] = a.astype(BF16)
            mixed[i + PIECES] = b.astype(BF16)
            split_pair(a, b, i, mkeep, msend)

    def mix_part(k):
        loop(4, lambda m: split_mixed(4 * k + m))
        mix_cores.start(k)
        loop(4, lambda m: pass_on(cstops, 1, 4 * k + m, csems))

    loop(4, mix_part)
    flip_out(mix_cores, mkeep, mstops, msems)

    def grad_mixed(n):
        for mode in range(2):
            i = 2 * n + mode
            relay_arrived(cstops, 2, (mode, n), csems)
            for h in range(2):
                ch = i + PIECES * h
                flat[pl.ds(pl.multiple_of(ch * R, R), R), :] = (
                    cot_in[ch].astype(F32) + c3[i, h].astype(F32))

    loop(PIECES // 2, grad_mixed)

    def grad_pre(i, total):
        g = (flat[pl.ds(i, C, stride=R), :] * slope[i]).astype(BF16)
        gs[1, i + 16] = g
        gzero[i + 16] = g
        return total + g.astype(F32)

    bias_total = lax.fori_loop(0, R, grad_pre, jnp.zeros((C, W), F32))
    ghalo.pack()
    ghalo.start()

    def weight_step(i):
        at = 8 + 4 * i
        g = jnp.concatenate([
            jnp.concatenate([gzero[at + k + D - D * p] for k in range(4)], axis=1) for p in range(3)], axis=0)
        v = jnp.concatenate([
            jnp.concatenate([xs[q, at + k] for k in range(4)], axis=1) for q in range(3)], axis=0)
        gsum[:, 0 : 3 * C] += lax.dot_general(g, v, (((1,), (1,)), ((), ())), preferred_element_type=F32)

    gsum[...] = jnp.zeros(gsum.shape, F32)
    loop(20, weight_step)
    lane = lanes((C, W))
    gsum[0:C, W : 2 * W] = jnp.where(
        lane < C, gsum[0:C, W : 2 * W], jnp.sum(bias_total, axis=1, keepdims=True))

    def piece(k):
        high, half = lax.div(k, 2), lax.rem(k, 2)
        return gsum.at[pl.ds(pl.multiple_of(high * 24, 8), 24), pl.ds(pl.multiple_of(half * W, W), W)]

    def rs_copy(k, slot, sem):
        return pltpu.make_async_remote_copy(
            piece(k), rs_in.at[slot], rs_ssem.at[k], rs_rsem.at[slot], device_id=(k, c), device_id_type=MESH)

    def ar_copy(k, slot):
        return pltpu.make_async_remote_copy(
            rs_mine, ar_in.at[slot], ar_ssem.at[k], ar_rsem.at[slot], device_id=(r, k), device_id_type=MESH)

    def ag_copy(k, slot):
        return pltpu.make_async_remote_copy(
            ag.at[r], ag.at[slot], ag_ssem.at[k], ag_rsem.at[slot], device_id=(k, c), device_id_type=MESH)

    others(16, r, lambda k: rs_copy(k, r, None).start())
    loop(PIECES // 2, lambda n: pass_on(mstops, 0, n, msems))
    ghalo.arrived()
    ghalo.shift()
    rs_in[r] = piece(r)[...]
    others(16, r, lambda k: rs_copy(k, k, None).wait_recv())
    rs_mine[...] = jnp.sum(rs_in[...], axis=0)
    others(8, c, lambda k: ar_copy(k, c).start())

    def backward(i):
        row = 4 * i
        back = jnp.dot(wb[:, 0 : 9 * C], tap_rows(gs, row, 4), preferred_element_type=F32)
        for k in range(4):
            flat[pl.ds(row + k, C, stride=R), :] = back[:, k * W : (k + 1) * W]

    loop(8, backward)
    ar_in[c] = rs_mine[...]
    others(8, c, lambda k: ar_copy(k, k).wait_recv())
    ag[r] = jnp.sum(ar_in[...], axis=0) * (1.0 / 1024)
    others(16, r, lambda k: ag_copy(k, r).start())
    loop(PIECES // 2, lambda n: pass_on(mstops, 1, n, msems))
    loop(8, lambda i: backward(i + 8))

    def input_out(i):
        for h in range(2):
            ch = i + PIECES * h
            gm = cot_in[ch].astype(F32) + c3[i, h].astype(F32)
            gin_ref[ch] = (gm + flat[pl.ds(pl.multiple_of(ch * R, R), R), :]).astype(BF16)

    loop(PIECES, input_out)

    def drain(stops, s, sems):
        def two(n):
            for mode in range(2):
                relay_sent(stops, s, (mode, n), sems)

        loop(PIECES // 2, two)

    cot_cores.sent()
    mix_cores.sent()
    xhalo.sent()
    ghalo.sent()
    for s in range(3):
        drain(cstops, s, csems)
    for s in range(2):
        drain(mstops, s, msems)
    others(16, r, lambda k: rs_copy(k, r, None).wait_send())
    others(8, c, lambda k: ar_copy(k, c).wait_send())
    others(16, r, lambda k: ag_copy(k, k).wait_recv())
    for k in range(16):
        gall[24 * (k // 2) : 24 * (k // 2) + 24, W * (k % 2) : W * (k % 2) + W] = ag[k]
    for p in range(3):
        two = gall[C * p : C * p + C, 0:W]
        gw_ref[p, 0] = two[:, 0:C]
        gw_ref[p, 1] = pltpu.roll(two, C, 1)[:, 0:C]
        gw_ref[p, 2] = gall[C * p : C * p + C, W : W + C]
    gb_ref[...] = jnp.transpose(gall[0:C, W : 2 * W], (1, 0))[C : C + 8, :]

    def sym_out(n):
        for mode in range(2):
            i = 2 * n + mode
            relay_arrived(mstops, 2, (mode, n), msems)
            for h in range(2):
                ch = i + PIECES * h
                sym_ref[ch] = (mixed[ch].astype(F32) + m3[i, h].astype(F32)).astype(BF16)

    loop(PIECES // 2, sym_out)
    drain(mstops, 2, msems)
    others(16, r, lambda k: ag_copy(k, r).wait_send())


def block(x, weight, bias, cot):
    vmem = pl.BlockSpec(memory_space=pltpu.VMEM)
    hbm = pl.BlockSpec(memory_space=pl.ANY)
    tile = pltpu.VMEM((C, R, W), BF16)
    stop = pltpu.VMEM((PIECES, 2, R, W), BF16)
    stack = pltpu.VMEM((3, R + 4 * D, C, W), BF16)
    pack, edge = pltpu.VMEM((2, 4, C, W), BF16), pltpu.VMEM((2, 6, C, W), BF16)
    weights = pltpu.VMEM((C, 640), BF16)
    dma = pltpu.SemaphoreType.DMA
    sym, gin, gw, gb = pl.pallas_call(
        kernel,
        out_shape=(
            jax.ShapeDtypeStruct((C, R, W), BF16),
            jax.ShapeDtypeStruct((C, R, W), BF16),
            jax.ShapeDtypeStruct((3, 3, C, C), F32),
            jax.ShapeDtypeStruct((8, C), F32),
        ),
        in_specs=[hbm, hbm, vmem, vmem],
        out_specs=[vmem] * 4,
        scratch_shapes=[
            tile, tile, weights, weights, pltpu.VMEM((C, W), F32),
            pltpu.VMEM((C * R, W), F32), stack, stack, pltpu.VMEM((R + 4 * D, C, W), BF16),
            pltpu.VMEM((R, C, W), F32), tile, pack, edge, pack, edge,
            pltpu.VMEM((PIECES, R, W), BF16), stop, stop, stop, stop, stop,
            pltpu.VMEM((PIECES, R, W), BF16), stop, stop, stop, stop, stop,
            pltpu.VMEM((3 * C, 2 * W), F32), pltpu.VMEM((3 * C, 2 * W), F32),
            pltpu.VMEM((16, 24, W), F32), pltpu.VMEM((24, W), F32),
            pltpu.VMEM((8, 24, W), F32), pltpu.VMEM((16, 24, W), F32),
            dma((2,)), dma((4,)), dma((4,)), dma((4,)), dma((4,)), dma((8,)), dma((8,)), dma((8,)), dma((8,)),
            dma((3, PIECES)), dma((3, PIECES)), dma((3, PIECES)), dma((3, PIECES)),
            dma((16,)), dma((16,)), dma((8,)), dma((8,)), dma((16,)), dma((16,)),
        ],
        compiler_params=pltpu.CompilerParams(
            collective_id=0, has_side_effects=True, vmem_limit_bytes=60 * 1024 * 1024),
    )(x, cot, weight, bias.reshape(1, C))
    return sym, gin, gw, gb[0]


def solution(mesh):
    tile = P(None, "row", "col")
    return jax.shard_map(
        block,
        mesh=mesh,
        in_specs=(tile, P(), P(), tile),
        out_specs=(tile, tile, P(), P()),
        check_vma=False,
    )
```

```python
import functools

import jax
import jax.numpy as jnp
from jax import lax
from jax.experimental import pallas as pl
from jax.experimental.pallas import tpu as pltpu
from jax.sharding import PartitionSpec as P

MESH = pl.DeviceIdType.MESH
F32 = jnp.float32
BF16 = jnp.bfloat16

C = 64
R = 64
W = 128
D = 8
PIECES = 32


def position():
    return lax.axis_index("row"), lax.axis_index("col")


def mod4(n):
    return lax.rem(n, 4)


def swap_middle(y):
    return jnp.where(jnp.logical_or(y == 1, y == 2), 3 - y, y)


def swap_outer(y):
    return jnp.where(jnp.logical_or(y == 0, y == 3), 3 - y, y)


def next_stop(stage, p):
    mode, n = p
    r, c = position()
    chip_row, core = lax.div(r, 2), lax.rem(r, 2)
    x, z = mod4(chip_row), mod4(c)
    y = 2 * lax.div(chip_row, 4) + lax.div(c, 4)
    k, how = lax.div(n, 4), lax.rem(n, 4)
    j = 2 * lax.rem(k, 2) + lax.div(k, 2)
    u, v = (z, x) if mode else (x, z)
    if stage == 0:
        u = mod4(u + v + j)
    elif stage == 1:
        v = mod4(u - j - v + 8)
    else:
        u = mod4(u - v - j + 8)
    nx, nz = (v, u) if mode else (u, v)
    around = swap_outer(y) if stage == 1 else y + 1 - 2 * lax.rem(y, 2)
    ny = jnp.where(how == 3, around, jnp.where(how == stage, swap_middle(y), y))
    nr = lax.div(ny, 2) * 8 + nx * 2 + core
    nc = lax.rem(ny, 2) * 4 + nz
    return nr, nc, jnp.logical_and(nr == r, nc == c)


def relay_copies(stops, s, p, sems):
    nr, nc, here = next_stop(s, p)
    r, _ = position()
    core = lax.rem(r, 2)
    mode, n = p
    i = 2 * n + mode
    ssem, rsem = sems

    def message(source, target, send, receive, row, there):
        remote = lambda: pltpu.make_async_remote_copy(
            source, target, ssem.at[send, i], rsem.at[receive, i], device_id=(row, nc), device_id_type=MESH)
        local = lambda: pltpu.make_async_copy(source, target, rsem.at[receive, i])
        return remote, local, there

    if s < 2:
        return [message(stops[s].at[i], stops[s + 1].at[i], s, s, nr, here)]
    return [message(stops[2].at[i, h], stops[3].at[i, core], 2 + h, 2 + core, nr - core + h,
                    jnp.logical_and(here, core == h)) for h in range(2)]


def relay_start(stops, s, p, sems):
    for remote, local, here in relay_copies(stops, s, p, sems):
        pl.when(here)(lambda: local().start())
        pl.when(jnp.logical_not(here))(lambda: remote().start())


def relay_arrived(stops, s, p, sems):
    i = 2 * p[1] + p[0]
    if s < 2:
        pltpu.make_async_copy(stops[s].at[i], stops[s + 1].at[i], sems[1].at[s, i]).wait()
    else:
        for core in range(2):
            pltpu.make_async_copy(stops[2].at[i, core], stops[3].at[i, core], sems[1].at[2 + core, i]).wait()


def relay_sent(stops, s, p, sems):
    for remote, _, here in relay_copies(stops, s, p, sems):
        pl.when(jnp.logical_not(here))(lambda: remote().wait_send())


def pass_on(stops, s, n, sems):
    for mode in range(2):
        relay_arrived(stops, s, (mode, n), sems)
        relay_start(stops, s + 1, (mode, n), sems)


def loop(n, body, by=1):
    def step(i, carry):
        for k in range(by):
            body(by * i + k)
        return carry

    lax.fori_loop(0, n // by, step, 0)


def lanes(shape):
    return lax.broadcasted_iota(jnp.int32, shape, 1)


class Halo:
    def __init__(self, stack, packed, edges, ssem, rsem):
        self.stack, self.edges, self.packed = stack, edges, packed
        self.sems = ssem, rsem
        r, c = position()
        up, down, left, right = r > 0, r < 15, c > 0, c < 7
        both = jnp.logical_and
        self.moves = [
            (stack.at[1, pl.ds(R + D, D)], stack.at[1, pl.ds(D, D)], 1, 0, down, up),
            (stack.at[1, pl.ds(2 * D, D)], stack.at[1, pl.ds(R + 2 * D, D)], -1, 0, up, down),
            (packed.at[1], edges.at[0, pl.ds(1, 4)], 0, 1, right, left),
            (packed.at[0], edges.at[1, pl.ds(1, 4)], 0, -1, left, right),
            (packed.at[1, 3], edges.at[0, 0], 1, 1, both(down, right), both(up, left)),
            (packed.at[0, 3], edges.at[1, 0], 1, -1, both(down, left), both(up, right)),
            (packed.at[1, 0], edges.at[0, 5], -1, 1, both(up, right), both(down, left)),
            (packed.at[0, 0], edges.at[1, 5], -1, -1, both(up, left), both(down, right)),
        ]

    def copy(self, k):
        r, c = position()
        source, target, dr, dc, _, _ = self.moves[k]
        ssem, rsem = self.sems
        return pltpu.make_async_remote_copy(
            source, target, ssem.at[k], rsem.at[k],
            device_id=(jnp.clip(r + dr, 0, 15), jnp.clip(c + dc, 0, 7)), device_id_type=MESH)

    def start(self):
        for k in range(8):
            pl.when(self.moves[k][4])(lambda: self.copy(k).start())

    def arrived(self, which):
        for k in which:
            pl.when(self.moves[k][5])(lambda: self.copy(k).wait_recv())

    def sent(self):
        for k in range(8):
            pl.when(self.moves[k][4])(lambda: self.copy(k).wait_send())

    def clear(self):
        stack, edges = self.stack, self.edges
        r, c = position()
        zero_rows = jnp.zeros((D, C, W), BF16)
        zero_corner = jnp.zeros((C, W), BF16)
        zero_cols = jnp.zeros(edges.shape[1:], BF16)

        @pl.when(r == 0)
        def _():
            stack[1, D : 2 * D] = zero_rows
            edges[0, 0] = zero_corner
            edges[1, 0] = zero_corner

        @pl.when(r == 15)
        def _():
            stack[1, R + 2 * D : R + 3 * D] = zero_rows
            edges[0, 5] = zero_corner
            edges[1, 5] = zero_corner

        @pl.when(c == 0)
        def _():
            edges[0] = zero_cols

        @pl.when(c == 7)
        def _():
            edges[1] = zero_cols

    def pack(self):
        stack, packed = self.stack, self.packed
        lane = lanes((C, W))

        def group(g):
            first = jnp.zeros((C, W), F32)
            last = jnp.zeros((C, W), F32)
            for k in range(16):
                v = stack[1, 16 * g + k + 16].astype(F32)
                mine = jnp.logical_and(lane >= 8 * k, lane < 8 * k + 8)
                first = jnp.where(mine, pltpu.roll(v, 8 * k, 1) if k else v, first)
                last = jnp.where(mine, pltpu.roll(v, (8 * k + 8) % W, 1) if k < 15 else v, last)
            packed[0, g] = first.astype(BF16)
            packed[1, g] = last.astype(BF16)

        loop(4, group)

    def columns_in(self):
        self.arrived((2, 3))
        self.shift(True)

    def rows_in(self):
        self.arrived((0, 1, 4, 5, 6, 7))
        self.shift(False)

    def shift(self, own):
        stack, edges = self.stack, self.edges
        lane = lanes((C, W))

        def eight(g, half):
            before = edges[0, g].astype(F32)
            after = edges[1, g].astype(F32)
            for k in range(8 * half, 8 * half + 8):
                v = stack[1, 16 * g + k].astype(F32)
                b = pltpu.roll(before, (W - 8 * k) % W, 1) if k else before
                a = pltpu.roll(after, (W - 8 - 8 * k) % W, 1) if k < 15 else after
                stack[0, 16 * g + k] = jnp.where(lane < D, b, pltpu.roll(v, D, 1)).astype(BF16)
                stack[2, 16 * g + k] = jnp.where(lane >= W - D, a, pltpu.roll(v, W - D, 1)).astype(BF16)

        def group(i):
            eight(i + 1, 0)
            eight(i + 1, 1)

        if own:
            loop(4, group)
        else:
            eight(0, 1)
            eight(5, 0)


def tap_rows(stack, row, count):
    parts = []
    for p in range(3):
        for q in range(3):
            parts.append(jnp.concatenate([stack[q, row + D + D * p + k] for k in range(count)], axis=1))
    return jnp.concatenate(parts, axis=0)


def flip(a, b):
    return jnp.transpose(jnp.concatenate([a, b], axis=0), (1, 0)).reshape(2, R, W)


def unfold(stop, i):
    lane = lanes((R, W))
    upper, lower = stop[i, 0].astype(F32), stop[i, 1].astype(F32)
    return (jnp.where(lane < C, upper, pltpu.roll(lower, C, 1)), jnp.where(lane < C, pltpu.roll(upper, C, 1), lower))


def others(n, me, body):
    def one(k):
        @pl.when(k != me)
        def _():
            body(k)

    loop(n, one)


def kernel(x_ref, cot_ref, w_ref, bias_ref, sym_ref, gin_ref, gw_ref, gb_ref,
           x_in, cot_in, wf, wb, bias2, flat, xs, gs, gzero, slope, mixed, xpack, xedge, gpack, gedge,
           c0, c1, c2, c3, m0, m1, m2, m3,
           gsum, gall, rs_in, rs_mine, ar_in, ag,
           in_sem, out_sem, xh_ssem, xh_rsem, gh_ssem, gh_rsem,
           c_ssem, c_rsem, m_ssem, m_rsem, rs_ssem, rs_rsem, ar_ssem, ar_rsem, ag_ssem, ag_rsem):
    r, c = position()
    barrier = pltpu.get_barrier_semaphore()
    greet = lambda nr, nc: pl.semaphore_signal(barrier, 1, device_id=(nr, nc), device_id_type=MESH)
    loop(32, lambda i: greet(lax.rem(i, 16), lax.div(i, 16) * 4 + mod4(c)), 4)
    own_half = mod4(lax.div(r, 2)) * 2 + lax.rem(r, 2)
    for k in range(1, 4):
        loop(4, lambda i: greet(lax.div(i, 2) * 8 + own_half, lax.rem(i, 2) * 4 + mod4(c + k)), 4)
    corners = [(dr, dc, jnp.logical_and(r + dr >= 0, r + dr < 16) & jnp.logical_and(c + dc >= 0, c + dc < 8))
               for dr in (-1, 1) for dc in (-1, 1)]
    for dr, dc, there in corners:
        pl.when(there)(lambda: greet(r + dr, c + dc))
    x_copy = pltpu.make_async_copy(x_ref, x_in, in_sem.at[0])
    cot_copy = pltpu.make_async_copy(cot_ref, cot_in, in_sem.at[1])
    cot_copy.start()
    x_copy.start()

    cstops, mstops = (c0, c1, c2, c3), (m0, m1, m2, m3)
    csems, msems = (c_ssem, c_rsem), (m_ssem, m_rsem)
    xhalo = Halo(xs, xpack, xedge, xh_ssem, xh_rsem)
    ghalo = Halo(gs, gpack, gedge, gh_ssem, gh_rsem)

    xhalo.clear()
    ghalo.clear()
    cot_copy.wait()

    def flip_cot(i):
        c0[i] = flip(cot_in[i], cot_in[i + PIECES])

    loop(PIECES, flip_cot, 2)
    x_copy.wait()

    def widen(i):
        flat[pl.ds(pl.multiple_of(i * R, R), R), :] = x_in[i].astype(F32)

    loop(C, widen, 4)

    def to_row(i):
        xs[1, i + 16] = flat[pl.ds(i, C, stride=R), :].astype(BF16)

    loop(R, to_row, 4)
    xhalo.pack()
    beside_r = 2 - (r == 0).astype(jnp.int32) - (r == 15).astype(jnp.int32)
    beside_c = 2 - (c == 0).astype(jnp.int32) - (c == 7).astype(jnp.int32)
    pl.semaphore_wait(barrier, 44 + beside_r * beside_c)
    xhalo.start()

    def cot_out(n):
        for mode in range(2):
            relay_start(cstops, 0, (mode, n), csems)

    loop(PIECES // 2, cot_out)
    spot = lax.broadcasted_iota(jnp.int32, (C, W), 0)
    left = (spot == lanes((C, W))).astype(BF16)
    right = (spot + C == lanes((C, W))).astype(BF16)
    for t in range(0, 9, 2):
        for out, at, dims in ((wf, lambda t: (t // 3, t % 3), ((1,), (0,))),
                              (wb, lambda t: (2 - t // 3, 2 - t % 3), ((0,), (0,)))):
            value = lax.dot_general(w_ref[at(t)], left, (dims, ((), ())), preferred_element_type=F32)
            if t < 8:
                value += lax.dot_general(w_ref[at(t + 1)], right, (dims, ((), ())), preferred_element_type=F32)
            out[:, C * t : C * t + W] = value.astype(BF16)
    bias2[...] = jnp.transpose(jnp.broadcast_to(bias_ref[...], (W, C)), (1, 0))

    gzero[0:16] = jnp.zeros((16, C, W), BF16)
    gzero[80:96] = jnp.zeros((16, C, W), BF16)
    loop(8, lambda n: pass_on(cstops, 0, n, csems))
    xhalo.columns_in()
    wide_bias = jnp.concatenate([bias2[...]] * 4, axis=1)

    def forward(i):
        row = 4 * i
        pre = jnp.dot(wf[:, 0 : 9 * C], tap_rows(xs, row, 4), preferred_element_type=F32) + wide_bias
        e = jnp.exp(jnp.minimum(pre, 0.0))
        up = pre > 0
        act = jnp.where(up, pre, e - 1.0)
        slp = jnp.where(up, 1.0, e)
        for k in range(4):
            at = slice(k * W, (k + 1) * W)
            value = xs[1, row + k + 16].astype(F32) + act[:, at]
            flat[pl.ds(row + k, C, stride=R), :] = value
            slope[row + k] = slp[:, at]

    def forward_and_pass(m):
        forward(m + 2)
        pass_on(cstops, 0, m + 8, csems)

    loop(8, forward_and_pass)
    loop(4, lambda m: forward(m + 10))
    xhalo.rows_in()
    for i in (0, 1, 14, 15):
        forward(i)

    def flip_mixed(n):
        for mode in range(2):
            i = 2 * n + mode
            a = flat[pl.ds(pl.multiple_of(i * R, R), R), :].astype(BF16)
            b = flat[pl.ds(pl.multiple_of((i + PIECES) * R, R), R), :].astype(BF16)
            mixed[i] = a
            mixed[i + PIECES] = b
            m0[i] = flip(a, b)

    def mix_out(n):
        for mode in range(2):
            relay_start(mstops, 0, (mode, n), msems)

    loop(PIECES // 2, flip_mixed)
    loop(8, lambda n: pass_on(cstops, 1, n, csems))
    loop(8, lambda n: pass_on(cstops, 1, n + 8, csems))
    loop(PIECES // 2, mix_out)

    def grad_mixed(n):
        for mode in range(2):
            i = 2 * n + mode
            relay_arrived(cstops, 2, (mode, n), csems)
            for h, flipped in enumerate(unfold(c3, i)):
                ch = i + PIECES * h
                flat[pl.ds(pl.multiple_of(ch * R, R), R), :] = cot_in[ch].astype(F32) + flipped
                c3[i, h] = flipped.astype(BF16)

    loop(PIECES // 2, grad_mixed)

    def grad_pre(i, total):
        g = (flat[pl.ds(i, C, stride=R), :] * slope[i]).astype(BF16)
        gs[1, i + 16] = g
        gzero[i + 16] = g
        return total + g.astype(F32)

    bias_total = lax.fori_loop(
        0, R // 4, lambda i, t: functools.reduce(lambda u, k: grad_pre(4 * i + k, u), range(4), t),
        jnp.zeros((C, W), F32))
    loop(8, lambda n: pass_on(mstops, 0, n, msems))

    def weight_step(i):
        at = 8 + 4 * i
        g = jnp.concatenate([
            jnp.concatenate([gzero[at + k + D - D * p] for k in range(4)], axis=1) for p in range(3)], axis=0)
        v = jnp.concatenate([
            jnp.concatenate([xs[q, at + k] for k in range(4)], axis=1) for q in range(3)], axis=0)
        gsum[:, 0 : 3 * C] += lax.dot_general(g, v, (((1,), (1,)), ((), ())), preferred_element_type=F32)

    gsum[...] = jnp.zeros(gsum.shape, F32)

    def weight_and_pass(n):
        weight_step(n)
        pass_on(mstops, 0, n + 8, msems)

    loop(8, weight_and_pass)
    loop(12, lambda i: weight_step(i + 8))
    lane = lanes((C, W))
    gsum[0:C, W : 2 * W] = jnp.where(
        lane < C, gsum[0:C, W : 2 * W], jnp.sum(bias_total, axis=1, keepdims=True))

    def piece(k):
        high, half = lax.div(k, 2), lax.rem(k, 2)
        return gsum.at[pl.ds(pl.multiple_of(high * 24, 8), 24), pl.ds(pl.multiple_of(half * W, W), W)]

    def rs_copy(k, slot, sem):
        return pltpu.make_async_remote_copy(
            piece(k), rs_in.at[slot], rs_ssem.at[k], rs_rsem.at[slot], device_id=(k, c), device_id_type=MESH)

    def ar_copy(k, slot):
        return pltpu.make_async_remote_copy(
            rs_mine, ar_in.at[slot], ar_ssem.at[k], ar_rsem.at[slot], device_id=(r, k), device_id_type=MESH)

    def ag_copy(k, slot):
        return pltpu.make_async_remote_copy(
            ag.at[r], ag.at[slot], ag_ssem.at[k], ag_rsem.at[slot], device_id=(k, c), device_id_type=MESH)

    def drain(stops, s, sems):
        def two(n):
            for mode in range(2):
                relay_sent(stops, s, (mode, n), sems)

        loop(PIECES // 2, two)

    others(16, r, lambda k: rs_copy(k, r, None).start())
    ghalo.pack()
    ghalo.start()
    loop(8, lambda n: pass_on(mstops, 1, n, msems))
    xhalo.sent()
    for s in range(3):
        drain(cstops, s, csems)
    rs_in[r] = piece(r)[...]
    others(16, r, lambda k: rs_copy(k, k, None).wait_recv())
    rs_mine[...] = jnp.sum(rs_in[...], axis=0)
    others(8, c, lambda k: ar_copy(k, c).start())
    loop(8, lambda n: pass_on(mstops, 1, n + 8, msems))
    ghalo.columns_in()

    def backward(i):
        row = 4 * i
        back = jnp.dot(wb[:, 0 : 9 * C], tap_rows(gs, row, 4), preferred_element_type=F32)
        for k in range(4):
            flat[pl.ds(row + k, C, stride=R), :] = back[:, k * W : (k + 1) * W]

    loop(4, lambda i: backward(i + 2))
    ar_in[c] = rs_mine[...]
    others(8, c, lambda k: ar_copy(k, k).wait_recv())
    ag[r] = jnp.sum(ar_in[...], axis=0) * (1.0 / 1024)
    others(16, r, lambda k: ag_copy(k, r).start())

    loop(8, lambda i: backward(i + 6))
    ghalo.rows_in()
    for i in (0, 1, 14, 15):
        backward(i)

    def input_out(i):
        for h in range(2):
            ch = i + PIECES * h
            gm = cot_in[ch].astype(F32) + c3[i, h].astype(F32)
            x_in[ch] = (gm + flat[pl.ds(pl.multiple_of(ch * R, R), R), :]).astype(BF16)

    loop(PIECES, input_out, 2)
    gin_copy = pltpu.make_async_copy(x_in, gin_ref, in_sem.at[0])
    gin_copy.start()

    ghalo.sent()
    for s in range(2):
        drain(mstops, s, msems)
    others(16, r, lambda k: rs_copy(k, r, None).wait_send())
    others(8, c, lambda k: ar_copy(k, c).wait_send())
    others(16, r, lambda k: ag_copy(k, k).wait_recv())
    for k in range(16):
        gall[24 * (k // 2) : 24 * (k // 2) + 24, W * (k % 2) : W * (k % 2) + W] = ag[k]
    for p in range(3):
        two = gall[C * p : C * p + C, 0:W]
        gw_ref[p, 0] = two[:, 0:C]
        gw_ref[p, 1] = pltpu.roll(two, C, 1)[:, 0:C]
        gw_ref[p, 2] = gall[C * p : C * p + C, W : W + C]
    gb_ref[...] = jnp.transpose(gall[0:C, W : 2 * W], (1, 0))[C : C + 1, :]

    def sym_out(n):
        for mode in range(2):
            i = 2 * n + mode
            relay_arrived(mstops, 2, (mode, n), msems)
            for h, flipped in enumerate(unfold(m3, i)):
                ch = i + PIECES * h
                mixed[ch] = (mixed[ch].astype(F32) + flipped).astype(BF16)

    def sym_copy(k, h):
        part = pl.ds(pl.multiple_of(8 * k + PIECES * h, 8), 8)
        return pltpu.make_async_copy(mixed.at[part], sym_ref.at[part], out_sem.at[2 * k + h])

    def sym_part(k):
        loop(4, lambda m: sym_out(4 * k + m))
        sym_copy(k, 0).start()
        sym_copy(k, 1).start()

    loop(4, sym_part)
    drain(mstops, 2, msems)
    gin_copy.wait()
    for k in range(4):
        sym_copy(k, 0).wait()
        sym_copy(k, 1).wait()
    others(16, r, lambda k: ag_copy(k, r).wait_send())


def place_kernel(*refs):
    n = (len(refs) - 2) // 3
    sources, targets, rooms, (came, went) = refs[:n], refs[n : 2 * n], refs[2 * n : 3 * n], refs[3 * n :]
    ins = [pltpu.make_async_copy(a, b, came.at[k]) for k, (a, b) in enumerate(zip(sources, rooms))]
    outs = [pltpu.make_async_copy(a, b, went.at[k]) for k, (a, b) in enumerate(zip(rooms, targets))]
    for copy in ins:
        copy.start()
    for arrived, copy in zip(ins, outs):
        arrived.wait()
        copy.start()
    for copy in outs:
        copy.wait()


def place(*arrays):
    hbm = pl.BlockSpec(memory_space=pl.ANY)
    n = len(arrays)
    return pl.pallas_call(
        place_kernel,
        out_shape=tuple(jax.ShapeDtypeStruct(a.shape, a.dtype) for a in arrays),
        in_specs=[hbm] * n,
        out_specs=(hbm,) * n,
        scratch_shapes=[pltpu.VMEM(a.shape, a.dtype) for a in arrays] + [pltpu.SemaphoreType.DMA((n,))] * 2,
        compiler_params=pltpu.CompilerParams(vmem_limit_bytes=60 * 1024 * 1024),
    )(*arrays)


def block(x, weight, bias, cot):
    vmem = pl.BlockSpec(memory_space=pltpu.VMEM)
    hbm = pl.BlockSpec(memory_space=pl.ANY)
    tile = pltpu.VMEM((C, R, W), BF16)
    stop = pltpu.VMEM((PIECES, 2, R, W), BF16)
    stack = pltpu.VMEM((3, R + 4 * D, C, W), BF16)
    pack, edge = pltpu.VMEM((2, 4, C, W), BF16), pltpu.VMEM((2, 6, C, W), BF16)
    weights = pltpu.VMEM((C, 640), BF16)
    dma = pltpu.SemaphoreType.DMA
    sym, gin, gw, gb = pl.pallas_call(
        kernel,
        out_shape=(
            jax.ShapeDtypeStruct((C, R, W), BF16),
            jax.ShapeDtypeStruct((C, R, W), BF16),
            jax.ShapeDtypeStruct((3, 3, C, C), F32),
            jax.ShapeDtypeStruct((1, C), F32),
        ),
        in_specs=[hbm, hbm, vmem, vmem],
        out_specs=[hbm, hbm, vmem, vmem],
        scratch_shapes=[
            tile, tile, weights, weights, pltpu.VMEM((C, W), F32),
            pltpu.VMEM((C * R, W), F32), stack, stack, pltpu.VMEM((R + 4 * D, C, W), BF16),
            pltpu.VMEM((R, C, W), F32), tile, pack, edge, pack, edge,
            stop, stop, stop, stop, stop, stop, stop, stop,
            pltpu.VMEM((3 * C, 2 * W), F32), pltpu.VMEM((3 * C, 2 * W), F32),
            pltpu.VMEM((16, 24, W), F32), pltpu.VMEM((24, W), F32),
            pltpu.VMEM((8, 24, W), F32), pltpu.VMEM((16, 24, W), F32),
            dma((2,)), dma((8,)), dma((8,)), dma((8,)), dma((8,)), dma((8,)),
            dma((4, PIECES)), dma((4, PIECES)), dma((4, PIECES)), dma((4, PIECES)),
            dma((16,)), dma((16,)), dma((8,)), dma((8,)), dma((16,)), dma((16,)),
        ],
        compiler_params=pltpu.CompilerParams(
            collective_id=0, has_side_effects=True, vmem_limit_bytes=60 * 1024 * 1024),
    )(x, cot, weight, bias.reshape(1, C))
    sym, gin, gw, gb = place(sym, gin, gw, gb)
    return sym, gin, gw, gb.reshape(C)


def solution(mesh):
    tile = P(None, "row", "col")
    return jax.shard_map(
        block,
        mesh=mesh,
        in_specs=(tile, P(), P(), tile),
        out_specs=(tile, tile, P(), P()),
        check_vma=False,
    )
```

```python
import functools

import jax
import jax.numpy as jnp
from jax import lax
from jax.experimental import pallas as pl
from jax.experimental.pallas import tpu as pltpu
from jax.sharding import PartitionSpec as P

MESH = pl.DeviceIdType.MESH
F32 = jnp.float32
BF16 = jnp.bfloat16

C = 64
R = 64
W = 128
D = 8
PIECES = 32


def position():
    return lax.axis_index("row"), lax.axis_index("col")


def mod4(n):
    return lax.rem(n, 4)


def swap_middle(y):
    return jnp.where(jnp.logical_or(y == 1, y == 2), 3 - y, y)


def swap_outer(y):
    return jnp.where(jnp.logical_or(y == 0, y == 3), 3 - y, y)


def next_stop(stage, p):
    mode, n = p
    r, c = position()
    chip_row, core = lax.div(r, 2), lax.rem(r, 2)
    x, z = mod4(chip_row), mod4(c)
    y = 2 * lax.div(chip_row, 4) + lax.div(c, 4)
    u, v = (z, x) if mode else (x, z)
    around = swap_outer(y) if stage == 1 else y + 1 - 2 * lax.rem(y, 2)
    if isinstance(n, int):
        j, how = 2 * (n // 4 % 2) + n // 8, n % 4
        ny = around if how == 3 else swap_middle(y) if how == stage else y
    else:
        j, how = 2 * lax.rem(lax.div(n, 4), 2) + lax.div(n, 8), lax.rem(n, 4)
        ny = jnp.where(how == 3, around, jnp.where(how == stage, swap_middle(y), y))
    if stage == 0:
        u = mod4(u + v + j)
    elif stage == 1:
        v = mod4(u - j - v + 8)
    else:
        u = mod4(u - v - j + 8)
    nx, nz = (v, u) if mode else (u, v)
    nr = lax.div(ny, 2) * 8 + nx * 2 + core
    nc = lax.rem(ny, 2) * 4 + nz
    return nr, nc, jnp.logical_and(nr == r, nc == c)


def relay_copies(stops, s, p, sems):
    nr, nc, here = next_stop(s, p)
    r, _ = position()
    core = lax.rem(r, 2)
    mode, n = p
    i = 2 * n + mode
    ssem, rsem = sems

    def message(source, target, send, receive, row, there):
        remote = lambda: pltpu.make_async_remote_copy(
            source, target, ssem.at[send, i], rsem.at[receive, i], device_id=(row, nc), device_id_type=MESH)
        local = lambda: pltpu.make_async_copy(source, target, rsem.at[receive, i])
        return remote, local, there

    if s < 2:
        return [message(stops[s].at[i], stops[s + 1].at[i], s, s, nr, here)]
    return [message(stops[2].at[i, h], stops[3].at[i, core], 2 + h, 2 + core, nr - core + h,
                    jnp.logical_and(here, core == h)) for h in range(2)]


def relay_start(stops, s, p, sems):
    for remote, local, here in relay_copies(stops, s, p, sems):
        pl.when(here)(lambda: local().start())
        pl.when(jnp.logical_not(here))(lambda: remote().start())


def relay_arrived(stops, s, p, sems):
    i = 2 * p[1] + p[0]
    if s < 2:
        pltpu.make_async_copy(stops[s].at[i], stops[s + 1].at[i], sems[1].at[s, i]).wait()
    else:
        for core in range(2):
            pltpu.make_async_copy(stops[2].at[i, core], stops[3].at[i, core], sems[1].at[2 + core, i]).wait()


def relay_sent(stops, s, p, sems):
    for remote, _, here in relay_copies(stops, s, p, sems):
        pl.when(jnp.logical_not(here))(lambda: remote().wait_send())


def pass_on(stops, s, n, sems):
    for mode in range(2):
        relay_arrived(stops, s, (mode, n), sems)
        relay_start(stops, s + 1, (mode, n), sems)


def loop(n, body, by=1):
    def step(i, carry):
        for k in range(by):
            body(by * i + k)
        return carry

    lax.fori_loop(0, n // by, step, 0)


def each(numbers, body):
    for n in numbers:
        body(n)


def lanes(shape):
    return lax.broadcasted_iota(jnp.int32, shape, 1)


class Halo:
    def __init__(self, stack, packed, edges, ssem, rsem):
        self.stack, self.edges, self.packed = stack, edges, packed
        self.sems = ssem, rsem
        r, c = position()
        up, down, left, right = r > 0, r < 15, c > 0, c < 7
        both = jnp.logical_and
        self.moves = [
            (stack.at[1, pl.ds(R + D, D)], stack.at[1, pl.ds(D, D)], 1, 0, down, up),
            (stack.at[1, pl.ds(2 * D, D)], stack.at[1, pl.ds(R + 2 * D, D)], -1, 0, up, down),
            (packed.at[1], edges.at[0, pl.ds(1, 4)], 0, 1, right, left),
            (packed.at[0], edges.at[1, pl.ds(1, 4)], 0, -1, left, right),
            (packed.at[1, 3], edges.at[0, 0], 1, 1, both(down, right), both(up, left)),
            (packed.at[0, 3], edges.at[1, 0], 1, -1, both(down, left), both(up, right)),
            (packed.at[1, 0], edges.at[0, 5], -1, 1, both(up, right), both(down, left)),
            (packed.at[0, 0], edges.at[1, 5], -1, -1, both(up, left), both(down, right)),
        ]

    def copy(self, k):
        r, c = position()
        source, target, dr, dc, _, _ = self.moves[k]
        ssem, rsem = self.sems
        return pltpu.make_async_remote_copy(
            source, target, ssem.at[k], rsem.at[k],
            device_id=(jnp.clip(r + dr, 0, 15), jnp.clip(c + dc, 0, 7)), device_id_type=MESH)

    def start(self):
        for k in range(8):
            pl.when(self.moves[k][4])(lambda: self.copy(k).start())

    def arrived(self, which):
        for k in which:
            pl.when(self.moves[k][5])(lambda: self.copy(k).wait_recv())

    def sent(self):
        for k in range(8):
            pl.when(self.moves[k][4])(lambda: self.copy(k).wait_send())

    def clear(self):
        stack, edges = self.stack, self.edges
        r, c = position()
        zero_rows = jnp.zeros((D, C, W), BF16)
        zero_corner = jnp.zeros((C, W), BF16)
        zero_cols = jnp.zeros(edges.shape[1:], BF16)

        @pl.when(r == 0)
        def _():
            stack[1, D : 2 * D] = zero_rows
            edges[0, 0] = zero_corner
            edges[1, 0] = zero_corner

        @pl.when(r == 15)
        def _():
            stack[1, R + 2 * D : R + 3 * D] = zero_rows
            edges[0, 5] = zero_corner
            edges[1, 5] = zero_corner

        @pl.when(c == 0)
        def _():
            edges[0] = zero_cols

        @pl.when(c == 7)
        def _():
            edges[1] = zero_cols

    def pack(self):
        stack, packed = self.stack, self.packed
        lane = lanes((C, W))

        def group(g):
            first = jnp.zeros((C, W), F32)
            last = jnp.zeros((C, W), F32)
            for k in range(16):
                v = stack[1, 16 * g + k + 16].astype(F32)
                mine = jnp.logical_and(lane >= 8 * k, lane < 8 * k + 8)
                first = jnp.where(mine, pltpu.roll(v, 8 * k, 1) if k else v, first)
                last = jnp.where(mine, pltpu.roll(v, (8 * k + 8) % W, 1) if k < 15 else v, last)
            packed[0, g] = first.astype(BF16)
            packed[1, g] = last.astype(BF16)

        loop(4, group)

    def columns_in(self):
        self.arrived((2, 3))
        self.shift(True)

    def rows_in(self):
        self.arrived((0, 1, 4, 5, 6, 7))
        self.shift(False)

    def shift(self, own):
        stack, edges = self.stack, self.edges
        lane = lanes((C, W))

        def eight(g, half):
            before = edges[0, g].astype(F32)
            after = edges[1, g].astype(F32)
            for k in range(8 * half, 8 * half + 8):
                v = stack[1, 16 * g + k].astype(F32)
                b = pltpu.roll(before, (W - 8 * k) % W, 1) if k else before
                a = pltpu.roll(after, (W - 8 - 8 * k) % W, 1) if k < 15 else after
                stack[0, 16 * g + k] = jnp.where(lane < D, b, pltpu.roll(v, D, 1)).astype(BF16)
                stack[2, 16 * g + k] = jnp.where(lane >= W - D, a, pltpu.roll(v, W - D, 1)).astype(BF16)

        def group(i):
            eight(i + 1, 0)
            eight(i + 1, 1)

        if own:
            loop(4, group)
        else:
            eight(0, 1)
            eight(5, 0)


def tap_rows(stack, row, count):
    parts = []
    for p in range(3):
        for q in range(3):
            parts.append(jnp.concatenate([stack[q, row + D + D * p + k] for k in range(count)], axis=1))
    return jnp.concatenate(parts, axis=0)


def flip(a, b):
    return jnp.transpose(jnp.concatenate([a, b], axis=0), (1, 0)).reshape(2, R, W)


def unfold(stop, i):
    lane = lanes((R, W))
    upper, lower = stop[i, 0].astype(F32), stop[i, 1].astype(F32)
    return (jnp.where(lane < C, upper, pltpu.roll(lower, C, 1)), jnp.where(lane < C, pltpu.roll(upper, C, 1), lower))


def others(n, me, body):
    for k in range(n):
        pl.when(k != me)(functools.partial(body, k))


def kernel(x_ref, cot_ref, w_ref, bias_ref, sym_ref, gin_ref, g_ref,
           x_in, cot_in, wf, wb, bias2, flat, xs, gs, gzero, slope, mixed, xpack, xedge, gpack, gedge,
           c0, c1, c2, c3, m0, m1, m2, m3,
           gsum, gall, rs_in, rs_mine, ar_in,
           in_sem, out_sem, xh_ssem, xh_rsem, gh_ssem, gh_rsem,
           c_ssem, c_rsem, m_ssem, m_rsem, rs_ssem, rs_rsem, ar_ssem, ar_rsem, ag_ssem, ag_rsem):
    r, c = position()
    barrier = pltpu.get_barrier_semaphore()
    greet = lambda nr, nc: pl.semaphore_signal(barrier, 1, device_id=(nr, nc), device_id_type=MESH)
    loop(32, lambda i: greet(lax.rem(i, 16), lax.div(i, 16) * 4 + mod4(c)), 4)
    own_half = mod4(lax.div(r, 2)) * 2 + lax.rem(r, 2)
    for k in range(1, 4):
        loop(4, lambda i: greet(lax.div(i, 2) * 8 + own_half, lax.rem(i, 2) * 4 + mod4(c + k)), 4)
    corners = [(dr, dc, jnp.logical_and(r + dr >= 0, r + dr < 16) & jnp.logical_and(c + dc >= 0, c + dc < 8))
               for dr in (-1, 1) for dc in (-1, 1)]
    for dr, dc, there in corners:
        pl.when(there)(lambda: greet(r + dr, c + dc))
    x_copy = pltpu.make_async_copy(x_ref, x_in, in_sem.at[0])
    cot_copy = pltpu.make_async_copy(cot_ref, cot_in, in_sem.at[1])
    cot_copy.start()
    x_copy.start()

    cstops, mstops = (c0, c1, c2, c3), (m0, m1, m2, m3)
    csems, msems = (c_ssem, c_rsem), (m_ssem, m_rsem)
    xhalo = Halo(xs, xpack, xedge, xh_ssem, xh_rsem)
    ghalo = Halo(gs, gpack, gedge, gh_ssem, gh_rsem)

    xhalo.clear()
    ghalo.clear()
    cot_copy.wait()

    def flip_cot(i):
        c0[i] = flip(cot_in[i], cot_in[i + PIECES])

    loop(PIECES, flip_cot, 2)
    x_copy.wait()

    def widen(i):
        flat[pl.ds(pl.multiple_of(i * R, R), R), :] = x_in[i].astype(F32)

    loop(C, widen, 4)

    def to_row(i):
        xs[1, i + 16] = flat[pl.ds(i, C, stride=R), :].astype(BF16)

    loop(R, to_row, 4)
    xhalo.pack()
    beside_r = 2 - (r == 0).astype(jnp.int32) - (r == 15).astype(jnp.int32)
    beside_c = 2 - (c == 0).astype(jnp.int32) - (c == 7).astype(jnp.int32)
    pl.semaphore_wait(barrier, 44 + beside_r * beside_c)
    xhalo.start()

    def cot_out(n):
        for mode in range(2):
            relay_start(cstops, 0, (mode, n), csems)

    each(range(16), cot_out)
    spot = lax.broadcasted_iota(jnp.int32, (C, W), 0)
    left = (spot == lanes((C, W))).astype(BF16)
    right = (spot + C == lanes((C, W))).astype(BF16)
    for t in range(0, 9, 2):
        for out, at, dims in ((wf, lambda t: (t // 3, t % 3), ((1,), (0,))),
                              (wb, lambda t: (2 - t // 3, 2 - t % 3), ((0,), (0,)))):
            value = lax.dot_general(w_ref[at(t)], left, (dims, ((), ())), preferred_element_type=F32)
            if t < 8:
                value += lax.dot_general(w_ref[at(t + 1)], right, (dims, ((), ())), preferred_element_type=F32)
            out[:, C * t : C * t + W] = value.astype(BF16)
    bias2[...] = jnp.transpose(jnp.broadcast_to(bias_ref[...], (W, C)), (1, 0))

    gzero[0:16] = jnp.zeros((16, C, W), BF16)
    gzero[80:96] = jnp.zeros((16, C, W), BF16)
    each(range(8), lambda n: pass_on(cstops, 0, n, csems))
    xhalo.columns_in()
    wide_bias = jnp.concatenate([bias2[...]] * 4, axis=1)

    def forward(i):
        row = 4 * i
        pre = jnp.dot(wf[:, 0 : 9 * C], tap_rows(xs, row, 4), preferred_element_type=F32) + wide_bias
        e = jnp.exp(jnp.minimum(pre, 0.0))
        up = pre > 0
        act = jnp.where(up, pre, e - 1.0)
        slp = jnp.where(up, 1.0, e)
        for k in range(4):
            at = slice(k * W, (k + 1) * W)
            value = xs[1, row + k + 16].astype(F32) + act[:, at]
            flat[pl.ds(row + k, C, stride=R), :] = value
            slope[row + k] = slp[:, at]

    def forward_and_pass(m):
        forward(m + 2)
        pass_on(cstops, 0, m + 8, csems)

    loop(8, forward_and_pass)
    loop(4, lambda m: forward(m + 10))
    xhalo.rows_in()
    for k, i in enumerate((0, 1, 14, 15)):
        forward(i)
        pass_on(cstops, 1, 2 * k, csems)
        pass_on(cstops, 1, 2 * k + 1, csems)
    each(range(8, 16), lambda n: pass_on(cstops, 1, n, csems))

    def flip_mixed(n):
        for mode in range(2):
            i = 2 * n + mode
            a = flat[pl.ds(pl.multiple_of(i * R, R), R), :].astype(BF16)
            b = flat[pl.ds(pl.multiple_of((i + PIECES) * R, R), R), :].astype(BF16)
            mixed[i] = a
            mixed[i + PIECES] = b
            m0[i] = flip(a, b)

    def mix_out(n):
        for mode in range(2):
            relay_start(mstops, 0, (mode, n), msems)

    loop(PIECES // 2, flip_mixed)
    each(range(16), mix_out)

    def grad_mixed(n):
        for mode in range(2):
            i = 2 * n + mode
            relay_arrived(cstops, 2, (mode, n), csems)
            for h, flipped in enumerate(unfold(c3, i)):
                ch = i + PIECES * h
                flat[pl.ds(pl.multiple_of(ch * R, R), R), :] = cot_in[ch].astype(F32) + flipped
                c3[i, h] = flipped.astype(BF16)

    loop(PIECES // 2, grad_mixed)

    def grad_pre(i, total):
        g = (flat[pl.ds(i, C, stride=R), :] * slope[i]).astype(BF16)
        gs[1, i + 16] = g
        gzero[i + 16] = g
        return total + g.astype(F32)

    bias_total = lax.fori_loop(
        0, R // 4, lambda i, t: functools.reduce(lambda u, k: grad_pre(4 * i + k, u), range(4), t),
        jnp.zeros((C, W), F32))
    each(range(16), lambda n: pass_on(mstops, 0, n, msems))

    def weight_step(i):
        at = 8 + 4 * i
        g = jnp.concatenate([
            jnp.concatenate([gzero[at + k + D - D * p] for k in range(4)], axis=1) for p in range(3)], axis=0)
        v = jnp.concatenate([
            jnp.concatenate([xs[q, at + k] for k in range(4)], axis=1) for q in range(3)], axis=0)
        gsum[:, 0 : 3 * C] += lax.dot_general(g, v, (((1,), (1,)), ((), ())), preferred_element_type=F32)

    gsum[...] = jnp.zeros(gsum.shape, F32)

    loop(20, weight_step)
    lane = lanes((C, W))
    gsum[0:C, W : 2 * W] = jnp.where(
        lane < C, gsum[0:C, W : 2 * W], jnp.sum(bias_total, axis=1, keepdims=True))

    def piece(k, whole=gsum):
        if isinstance(k, int):
            return whole.at[24 * (k // 2) : 24 * (k // 2) + 24, W * (k % 2) : W * (k % 2) + W]
        return whole.at[pl.ds(pl.multiple_of(lax.div(k, 2) * 24, 8), 24), pl.ds(pl.multiple_of(lax.rem(k, 2) * W, W), W)]

    high, low = lax.div(r, 8), lax.div(c, 4)
    near, far = low * 8 + lax.rem(r, 8), high * 4 + mod4(c)

    def near_id(k):
        return high * 8 + k % 8, k // 8 * 4 + mod4(c)

    def far_id(k):
        return k // 4 * 8 + lax.rem(r, 8), low * 4 + k % 4

    def rs_copy(k, slot):
        return pltpu.make_async_remote_copy(
            piece(k), rs_in.at[slot], rs_ssem.at[k], rs_rsem.at[slot], device_id=near_id(k), device_id_type=MESH)

    def ar_copy(k, slot):
        return pltpu.make_async_remote_copy(
            rs_mine, ar_in.at[slot], ar_ssem.at[k], ar_rsem.at[slot], device_id=far_id(k), device_id_type=MESH)

    def ag_copy(k, slot):
        return pltpu.make_async_remote_copy(
            piece(near, gall), piece(slot, gall), ag_ssem.at[k], ag_rsem.at[slot], device_id=near_id(k), device_id_type=MESH)

    def drain(stops, s, sems):
        for n in range(PIECES // 2):
            for mode in range(2):
                relay_sent(stops, s, (mode, n), sems)

    others(16, near, lambda k: rs_copy(k, near).start())
    ghalo.pack()
    ghalo.start()
    each(range(8), lambda n: pass_on(mstops, 1, n, msems))
    xhalo.sent()
    for s in range(3):
        drain(cstops, s, csems)
    rs_in[near] = piece(near)[...]
    others(16, near, lambda k: rs_copy(k, k).wait_recv())
    rs_mine[...] = jnp.sum(rs_in[...], axis=0)
    others(8, far, lambda k: ar_copy(k, far).start())
    each(range(8, 16), lambda n: pass_on(mstops, 1, n, msems))
    ghalo.columns_in()

    def backward(i):
        row = 4 * i
        back = jnp.dot(wb[:, 0 : 9 * C], tap_rows(gs, row, 4), preferred_element_type=F32)
        for k in range(4):
            flat[pl.ds(row + k, C, stride=R), :] = back[:, k * W : (k + 1) * W]

    loop(8, lambda i: backward(i + 2))
    ar_in[far] = rs_mine[...]
    others(8, far, lambda k: ar_copy(k, k).wait_recv())
    piece(near, gall)[...] = jnp.sum(ar_in[...], axis=0) * (1.0 / 1024)
    others(16, near, lambda k: ag_copy(k, near).start())

    loop(4, lambda i: backward(i + 10))
    ghalo.rows_in()
    for i in (0, 1, 14, 15):
        backward(i)

    def input_out(i):
        for h in range(2):
            ch = i + PIECES * h
            gm = cot_in[ch].astype(F32) + c3[i, h].astype(F32)
            x_in[ch] = (gm + flat[pl.ds(pl.multiple_of(ch * R, R), R), :]).astype(BF16)

    loop(PIECES, input_out, 2)
    gin_copy = pltpu.make_async_copy(x_in, gin_ref, in_sem.at[0])
    gin_copy.start()

    ghalo.sent()
    for s in range(2):
        drain(mstops, s, msems)
    others(16, near, lambda k: rs_copy(k, near).wait_send())
    others(8, far, lambda k: ar_copy(k, far).wait_send())

    def sym_out(n):
        for mode in range(2):
            i = 2 * n + mode
            relay_arrived(mstops, 2, (mode, n), msems)
            for h, flipped in enumerate(unfold(m3, i)):
                ch = i + PIECES * h
                mixed[ch] = (mixed[ch].astype(F32) + flipped).astype(BF16)

    def sym_copy(k, h):
        part = pl.ds(pl.multiple_of(8 * k + PIECES * h, 8), 8)
        return pltpu.make_async_copy(mixed.at[part], sym_ref.at[part], out_sem.at[2 * k + h])

    def sym_part(k):
        loop(4, lambda m: sym_out(4 * k + m))
        sym_copy(k, 0).start()
        sym_copy(k, 1).start()

    loop(4, sym_part)
    drain(mstops, 2, msems)
    others(16, near, lambda k: ag_copy(k, k).wait_recv())
    g_copy = pltpu.make_async_copy(gall, g_ref, in_sem.at[1])
    g_copy.start()
    gin_copy.wait()
    g_copy.wait()
    for k in range(4):
        sym_copy(k, 0).wait()
        sym_copy(k, 1).wait()
    others(16, near, lambda k: ag_copy(k, near).wait_send())


def place_kernel(sym_ref, gin_ref, g_ref, sym_out, gin_out, gw_out, gb_out, sym, gin, grads, gw, came, went):
    g_in = pltpu.make_async_copy(g_ref, grads, came.at[4])
    g_in.start()
    ins, outs = [], []
    for k in range(2):
        part = pl.ds(k * C // 2, C // 2)
        for n, (a, b, room) in enumerate(((sym_ref, sym_out, sym), (gin_ref, gin_out, gin))):
            ins.append(pltpu.make_async_copy(a.at[part], room.at[part], came.at[2 * k + n]))
            outs.append(pltpu.make_async_copy(room.at[part], b.at[part], went.at[2 * k + n]))
    for copy in ins:
        copy.start()
    g_in.wait()
    for p in range(3):
        two = grads[C * p : C * p + C, 0:W]
        gw[p, 0] = two[:, 0:C]
        gw[p, 1] = pltpu.roll(two, C, 1)[:, 0:C]
        gw[p, 2] = grads[C * p : C * p + C, W : W + C]
    gw_copy = pltpu.make_async_copy(gw, gw_out, went.at[4])
    gw_copy.start()
    outs.append(gw_copy)
    gb_out[...] = jnp.transpose(grads[0:C, W : 2 * W], (1, 0))[C : C + 1, :]
    for arrived, copy in zip(ins, outs):
        arrived.wait()
        copy.start()
    for copy in outs:
        copy.wait()


def place(sym, gin, grads):
    hbm = pl.BlockSpec(memory_space=pl.ANY)
    vmem = pl.BlockSpec(memory_space=pltpu.VMEM)
    tile = pltpu.VMEM((C, R, W), BF16)
    return pl.pallas_call(
        place_kernel,
        out_shape=(
            jax.ShapeDtypeStruct((C, R, W), BF16),
            jax.ShapeDtypeStruct((C, R, W), BF16),
            jax.ShapeDtypeStruct((3, 3, C, C), F32),
            jax.ShapeDtypeStruct((1, C), F32),
        ),
        in_specs=[hbm] * 3,
        out_specs=(hbm, hbm, hbm, vmem),
        scratch_shapes=[
            tile, tile, pltpu.VMEM((3 * C, 2 * W), F32), pltpu.VMEM((3, 3, C, C), F32),
            pltpu.SemaphoreType.DMA((5,)), pltpu.SemaphoreType.DMA((5,))],
        compiler_params=pltpu.CompilerParams(vmem_limit_bytes=60 * 1024 * 1024),
    )(sym, gin, grads)


def block(x, weight, bias, cot):
    vmem = pl.BlockSpec(memory_space=pltpu.VMEM)
    hbm = pl.BlockSpec(memory_space=pl.ANY)
    tile = pltpu.VMEM((C, R, W), BF16)
    stop = pltpu.VMEM((PIECES, 2, R, W), BF16)
    stack = pltpu.VMEM((3, R + 4 * D, C, W), BF16)
    pack, edge = pltpu.VMEM((2, 4, C, W), BF16), pltpu.VMEM((2, 6, C, W), BF16)
    weights = pltpu.VMEM((C, 640), BF16)
    dma = pltpu.SemaphoreType.DMA
    sym, gin, grads = pl.pallas_call(
        kernel,
        out_shape=(
            jax.ShapeDtypeStruct((C, R, W), BF16),
            jax.ShapeDtypeStruct((C, R, W), BF16),
            jax.ShapeDtypeStruct((3 * C, 2 * W), F32),
        ),
        in_specs=[hbm, hbm, vmem, vmem],
        out_specs=[hbm] * 3,
        scratch_shapes=[
            tile, tile, weights, weights, pltpu.VMEM((C, W), F32),
            pltpu.VMEM((C * R, W), F32), stack, stack, pltpu.VMEM((R + 4 * D, C, W), BF16),
            pltpu.VMEM((R, C, W), F32), tile, pack, edge, pack, edge,
            stop, stop, stop, stop, stop, stop, stop, stop,
            pltpu.VMEM((3 * C, 2 * W), F32), pltpu.VMEM((3 * C, 2 * W), F32),
            pltpu.VMEM((16, 24, W), F32), pltpu.VMEM((24, W), F32),
            pltpu.VMEM((8, 24, W), F32),
            dma((2,)), dma((8,)), dma((8,)), dma((8,)), dma((8,)), dma((8,)),
            dma((4, PIECES)), dma((4, PIECES)), dma((4, PIECES)), dma((4, PIECES)),
            dma((16,)), dma((16,)), dma((8,)), dma((8,)), dma((16,)), dma((16,)),
        ],
        compiler_params=pltpu.CompilerParams(
            collective_id=0, has_side_effects=True, vmem_limit_bytes=60 * 1024 * 1024),
    )(x, cot, weight, bias.reshape(1, C))
    sym, gin, gw, gb = place(sym, gin, grads)
    return sym, gin, gw, gb.reshape(C)


def solution(mesh):
    tile = P(None, "row", "col")
    return jax.shard_map(
        block,
        mesh=mesh,
        in_specs=(tile, P(), P(), tile),
        out_specs=(tile, tile, P(), P()),
        check_vma=False,
    )
```

```python
import functools

import jax
import jax.numpy as jnp
from jax import lax
from jax.experimental import pallas as pl
from jax.experimental.pallas import tpu as pltpu
from jax.sharding import PartitionSpec as P

MESH = pl.DeviceIdType.MESH
F32 = jnp.float32
BF16 = jnp.bfloat16

C = 64
R = 64
W = 128
D = 8
PIECES = 32


def position():
    return lax.axis_index("row"), lax.axis_index("col")


def mod4(n):
    return lax.rem(n, 4)


def swap_middle(y):
    return jnp.where(jnp.logical_or(y == 1, y == 2), 3 - y, y)


def swap_outer(y):
    return jnp.where(jnp.logical_or(y == 0, y == 3), 3 - y, y)


def next_stop(stage, p):
    mode, n = p
    r, c = position()
    chip_row, core = lax.div(r, 2), lax.rem(r, 2)
    x, z = mod4(chip_row), mod4(c)
    y = 2 * lax.div(chip_row, 4) + lax.div(c, 4)
    u, v = (z, x) if mode else (x, z)
    around = swap_outer(y) if stage == 1 else y + 1 - 2 * lax.rem(y, 2)
    if isinstance(n, int):
        j, how = 2 * (n // 4 % 2) + n // 8, n % 4
        ny = around if how == 3 else swap_middle(y) if how == stage else y
    else:
        j, how = 2 * lax.rem(lax.div(n, 4), 2) + lax.div(n, 8), lax.rem(n, 4)
        ny = jnp.where(how == 3, around, jnp.where(how == stage, swap_middle(y), y))
    if stage == 0:
        u = mod4(u + v + j)
    elif stage == 1:
        v = mod4(u - j - v + 8)
    else:
        u = mod4(u - v - j + 8)
    nx, nz = (v, u) if mode else (u, v)
    nr = lax.div(ny, 2) * 8 + nx * 2 + core
    nc = lax.rem(ny, 2) * 4 + nz
    return nr, nc, jnp.logical_and(nr == r, nc == c)


def relay_copies(stops, s, p, sems):
    nr, nc, here = next_stop(s, p)
    r, _ = position()
    core = lax.rem(r, 2)
    mode, n = p
    i = 2 * n + mode
    ssem, rsem = sems

    def message(source, target, send, receive, row, there):
        remote = lambda: pltpu.make_async_remote_copy(
            source, target, ssem.at[send, i], rsem.at[receive, i], device_id=(row, nc), device_id_type=MESH)
        local = lambda: pltpu.make_async_copy(source, target, rsem.at[receive, i])
        return remote, local, there

    if s < 2:
        return [message(stops[s].at[i], stops[s + 1].at[i], s, s, nr, here)]
    return [message(stops[2].at[i, h], stops[3].at[i, core], 2 + h, 2 + core, nr - core + h,
                    jnp.logical_and(here, core == h)) for h in range(2)]


def relay_start(stops, s, p, sems):
    for remote, local, here in relay_copies(stops, s, p, sems):
        pl.when(here)(lambda: local().start())
        pl.when(jnp.logical_not(here))(lambda: remote().start())


def relay_arrived(stops, s, p, sems):
    i = 2 * p[1] + p[0]
    if s < 2:
        pltpu.make_async_copy(stops[s].at[i], stops[s + 1].at[i], sems[1].at[s, i]).wait()
    else:
        for core in range(2):
            pltpu.make_async_copy(stops[2].at[i, core], stops[3].at[i, core], sems[1].at[2 + core, i]).wait()


def relay_sent(stops, s, p, sems):
    for remote, _, here in relay_copies(stops, s, p, sems):
        pl.when(jnp.logical_not(here))(lambda: remote().wait_send())


def pass_on(stops, s, n, sems):
    for mode in range(2):
        relay_arrived(stops, s, (mode, n), sems)
        relay_start(stops, s + 1, (mode, n), sems)


def loop(n, body, by=1):
    def step(i, carry):
        for k in range(by):
            body(by * i + k)
        return carry

    lax.fori_loop(0, n // by, step, 0)


def each(numbers, body):
    for n in numbers:
        body(n)


def lanes(shape):
    return lax.broadcasted_iota(jnp.int32, shape, 1)


class Halo:
    def __init__(self, stack, packed, edges, ssem, rsem):
        self.stack, self.edges, self.packed = stack, edges, packed
        self.sems = ssem, rsem
        r, c = position()
        up, down, left, right = r > 0, r < 15, c > 0, c < 7
        both = jnp.logical_and
        self.moves = [
            (stack.at[1, pl.ds(R + D, D)], stack.at[1, pl.ds(D, D)], 1, 0, down, up),
            (stack.at[1, pl.ds(2 * D, D)], stack.at[1, pl.ds(R + 2 * D, D)], -1, 0, up, down),
            (packed.at[1], edges.at[0, pl.ds(1, 4)], 0, 1, right, left),
            (packed.at[0], edges.at[1, pl.ds(1, 4)], 0, -1, left, right),
            (packed.at[1, 3], edges.at[0, 0], 1, 1, both(down, right), both(up, left)),
            (packed.at[0, 3], edges.at[1, 0], 1, -1, both(down, left), both(up, right)),
            (packed.at[1, 0], edges.at[0, 5], -1, 1, both(up, right), both(down, left)),
            (packed.at[0, 0], edges.at[1, 5], -1, -1, both(up, left), both(down, right)),
        ]

    def copy(self, k):
        r, c = position()
        source, target, dr, dc, _, _ = self.moves[k]
        ssem, rsem = self.sems
        return pltpu.make_async_remote_copy(
            source, target, ssem.at[k], rsem.at[k],
            device_id=(jnp.clip(r + dr, 0, 15), jnp.clip(c + dc, 0, 7)), device_id_type=MESH)

    def start(self):
        for k in range(8):
            pl.when(self.moves[k][4])(lambda: self.copy(k).start())

    def arrived(self, which):
        for k in which:
            pl.when(self.moves[k][5])(lambda: self.copy(k).wait_recv())

    def sent(self):
        for k in range(8):
            pl.when(self.moves[k][4])(lambda: self.copy(k).wait_send())

    def clear(self):
        stack, edges = self.stack, self.edges
        r, c = position()
        zero_rows = jnp.zeros((D, C, W), BF16)
        zero_corner = jnp.zeros((C, W), BF16)
        zero_cols = jnp.zeros(edges.shape[1:], BF16)

        @pl.when(r == 0)
        def _():
            stack[1, D : 2 * D] = zero_rows
            edges[0, 0] = zero_corner
            edges[1, 0] = zero_corner

        @pl.when(r == 15)
        def _():
            stack[1, R + 2 * D : R + 3 * D] = zero_rows
            edges[0, 5] = zero_corner
            edges[1, 5] = zero_corner

        @pl.when(c == 0)
        def _():
            edges[0] = zero_cols

        @pl.when(c == 7)
        def _():
            edges[1] = zero_cols

    def pack(self):
        stack, packed = self.stack, self.packed
        lane = lanes((C, W))

        def group(g):
            first = jnp.zeros((C, W), F32)
            last = jnp.zeros((C, W), F32)
            for k in range(16):
                v = stack[1, 16 * g + k + 16].astype(F32)
                mine = jnp.logical_and(lane >= 8 * k, lane < 8 * k + 8)
                first = jnp.where(mine, pltpu.roll(v, 8 * k, 1) if k else v, first)
                last = jnp.where(mine, pltpu.roll(v, (8 * k + 8) % W, 1) if k < 15 else v, last)
            packed[0, g] = first.astype(BF16)
            packed[1, g] = last.astype(BF16)

        loop(4, group)

    def columns_in(self):
        self.arrived((2, 3))
        self.shift(True)

    def rows_in(self):
        self.arrived((0, 1, 4, 5, 6, 7))
        self.shift(False)

    def shift(self, own):
        stack, edges = self.stack, self.edges
        lane = lanes((C, W))

        def eight(g, half):
            before = edges[0, g].astype(F32)
            after = edges[1, g].astype(F32)
            for k in range(8 * half, 8 * half + 8):
                v = stack[1, 16 * g + k].astype(F32)
                b = pltpu.roll(before, (W - 8 * k) % W, 1) if k else before
                a = pltpu.roll(after, (W - 8 - 8 * k) % W, 1) if k < 15 else after
                stack[0, 16 * g + k] = jnp.where(lane < D, b, pltpu.roll(v, D, 1)).astype(BF16)
                stack[2, 16 * g + k] = jnp.where(lane >= W - D, a, pltpu.roll(v, W - D, 1)).astype(BF16)

        def group(i):
            eight(i + 1, 0)
            eight(i + 1, 1)

        if own:
            loop(4, group)
        else:
            eight(0, 1)
            eight(5, 0)


def tap_rows(stack, row, count):
    parts = []
    for p in range(3):
        for q in range(3):
            parts.append(jnp.concatenate([stack[q, row + D + D * p + k] for k in range(count)], axis=1))
    return jnp.concatenate(parts, axis=0)


def flip(a, b):
    return jnp.transpose(jnp.concatenate([a, b], axis=0), (1, 0)).reshape(2, R, W)


def unfold(stop, i):
    lane = lanes((R, W))
    upper, lower = stop[i, 0].astype(F32), stop[i, 1].astype(F32)
    return (jnp.where(lane < C, upper, pltpu.roll(lower, C, 1)), jnp.where(lane < C, pltpu.roll(upper, C, 1), lower))


def others(n, me, body):
    for k in range(n):
        pl.when(k != me)(functools.partial(body, k))


def kernel(x_ref, cot_ref, w_ref, bias_ref, sym_ref, gin_ref, g_ref,
           x_in, cot_in, wf, wb, bias2, flat, xs, gs, gzero, slope, mixed, xpack, xedge, gpack, gedge,
           c0, c1, c2, c3, m0, m1, m2, m3,
           gsum, gall, rs_in, rs_mine, ar_in,
           in_sem, out_sem, xh_ssem, xh_rsem, gh_ssem, gh_rsem,
           c_ssem, c_rsem, m_ssem, m_rsem, rs_ssem, rs_rsem, ar_ssem, ar_rsem, ag_ssem, ag_rsem):
    r, c = position()
    barrier = pltpu.get_barrier_semaphore()
    greet = lambda nr, nc: pl.semaphore_signal(barrier, 1, device_id=(nr, nc), device_id_type=MESH)
    loop(32, lambda i: greet(lax.rem(i, 16), lax.div(i, 16) * 4 + mod4(c)), 4)
    own_half = mod4(lax.div(r, 2)) * 2 + lax.rem(r, 2)
    for k in range(1, 4):
        loop(4, lambda i: greet(lax.div(i, 2) * 8 + own_half, lax.rem(i, 2) * 4 + mod4(c + k)), 4)
    corners = [(dr, dc, jnp.logical_and(r + dr >= 0, r + dr < 16) & jnp.logical_and(c + dc >= 0, c + dc < 8))
               for dr in (-1, 1) for dc in (-1, 1)]
    for dr, dc, there in corners:
        pl.when(there)(lambda: greet(r + dr, c + dc))
    x_copy = pltpu.make_async_copy(x_ref, x_in, in_sem.at[0])
    cot_copy = pltpu.make_async_copy(cot_ref, cot_in, in_sem.at[1])
    cot_copy.start()
    x_copy.start()

    cstops, mstops = (c0, c1, c2, c3), (m0, m1, m2, m3)
    csems, msems = (c_ssem, c_rsem), (m_ssem, m_rsem)
    xhalo = Halo(xs, xpack, xedge, xh_ssem, xh_rsem)
    ghalo = Halo(gs, gpack, gedge, gh_ssem, gh_rsem)

    xhalo.clear()
    ghalo.clear()
    cot_copy.wait()

    def flip_cot(i):
        c0[i] = flip(cot_in[i], cot_in[i + PIECES])

    loop(PIECES, flip_cot, 2)
    beside_r = 2 - (r == 0).astype(jnp.int32) - (r == 15).astype(jnp.int32)
    beside_c = 2 - (c == 0).astype(jnp.int32) - (c == 7).astype(jnp.int32)
    pl.semaphore_wait(barrier, 44 + beside_r * beside_c)
    def cot_out(n):
        for mode in range(2):
            relay_start(cstops, 0, (mode, n), csems)

    each(range(8), cot_out)
    x_copy.wait()

    def widen(i):
        flat[pl.ds(pl.multiple_of(i * R, R), R), :] = x_in[i].astype(F32)

    loop(C, widen, 4)

    def to_row(i):
        xs[1, i + 16] = flat[pl.ds(i, C, stride=R), :].astype(BF16)

    loop(R, to_row, 4)
    xhalo.pack()
    xhalo.start()

    each(range(8, 16), cot_out)
    spot = lax.broadcasted_iota(jnp.int32, (C, W), 0)
    left = (spot == lanes((C, W))).astype(BF16)
    right = (spot + C == lanes((C, W))).astype(BF16)
    for t in range(0, 9, 2):
        for out, at, dims in ((wf, lambda t: (t // 3, t % 3), ((1,), (0,))),
                              (wb, lambda t: (2 - t // 3, 2 - t % 3), ((0,), (0,)))):
            value = lax.dot_general(w_ref[at(t)], left, (dims, ((), ())), preferred_element_type=F32)
            if t < 8:
                value += lax.dot_general(w_ref[at(t + 1)], right, (dims, ((), ())), preferred_element_type=F32)
            out[:, C * t : C * t + W] = value.astype(BF16)
    bias2[...] = jnp.transpose(jnp.broadcast_to(bias_ref[...], (W, C)), (1, 0))

    gzero[0:16] = jnp.zeros((16, C, W), BF16)
    gzero[80:96] = jnp.zeros((16, C, W), BF16)
    each(range(8), lambda n: pass_on(cstops, 0, n, csems))
    xhalo.columns_in()
    wide_bias = jnp.concatenate([bias2[...]] * 4, axis=1)

    def forward(i):
        row = 4 * i
        pre = jnp.dot(wf[:, 0 : 9 * C], tap_rows(xs, row, 4), preferred_element_type=F32) + wide_bias
        e = jnp.exp(jnp.minimum(pre, 0.0))
        up = pre > 0
        act = jnp.where(up, pre, e - 1.0)
        slp = jnp.where(up, 1.0, e)
        for k in range(4):
            at = slice(k * W, (k + 1) * W)
            value = xs[1, row + k + 16].astype(F32) + act[:, at]
            flat[pl.ds(row + k, C, stride=R), :] = value
            slope[row + k] = slp[:, at]

    def forward_and_pass(m):
        forward(m + 2)
        pass_on(cstops, 0, m + 8, csems)

    loop(8, forward_and_pass)
    loop(4, lambda m: forward(m + 10))
    xhalo.rows_in()
    for k, i in enumerate((0, 1, 14, 15)):
        forward(i)
        pass_on(cstops, 1, 2 * k, csems)
        pass_on(cstops, 1, 2 * k + 1, csems)

    def flip_mixed(n):
        for mode in range(2):
            i = 2 * n + mode
            a = flat[pl.ds(pl.multiple_of(i * R, R), R), :].astype(BF16)
            b = flat[pl.ds(pl.multiple_of((i + PIECES) * R, R), R), :].astype(BF16)
            mixed[i] = a
            mixed[i + PIECES] = b
            m0[i] = flip(a, b)

    def mix_out(n):
        for mode in range(2):
            relay_start(mstops, 0, (mode, n), msems)

    loop(PIECES // 2, flip_mixed)
    each(range(8, 16), lambda n: pass_on(cstops, 1, n, csems))
    each(range(16), mix_out)

    def grad_mixed(n):
        for mode in range(2):
            i = 2 * n + mode
            relay_arrived(cstops, 2, (mode, n), csems)
            for h, flipped in enumerate(unfold(c3, i)):
                ch = i + PIECES * h
                flat[pl.ds(pl.multiple_of(ch * R, R), R), :] = cot_in[ch].astype(F32) + flipped
                c3[i, h] = flipped.astype(BF16)

    loop(PIECES // 2, grad_mixed)

    def grad_pre(i, total):
        g = (flat[pl.ds(i, C, stride=R), :] * slope[i]).astype(BF16)
        gs[1, i + 16] = g
        gzero[i + 16] = g
        return total + g.astype(F32)

    bias_total = lax.fori_loop(
        0, R // 4, lambda i, t: functools.reduce(lambda u, k: grad_pre(4 * i + k, u), range(4), t),
        jnp.zeros((C, W), F32))
    each(range(16), lambda n: pass_on(mstops, 0, n, msems))

    def weight_step(i):
        at = 8 + 4 * i
        g = jnp.concatenate([
            jnp.concatenate([gzero[at + k + D - D * p] for k in range(4)], axis=1) for p in range(3)], axis=0)
        v = jnp.concatenate([
            jnp.concatenate([xs[q, at + k] for k in range(4)], axis=1) for q in range(3)], axis=0)
        gsum[:, 0 : 3 * C] += lax.dot_general(g, v, (((1,), (1,)), ((), ())), preferred_element_type=F32)

    gsum[...] = jnp.zeros(gsum.shape, F32)

    loop(20, weight_step)
    lane = lanes((C, W))
    gsum[0:C, W : 2 * W] = jnp.where(
        lane < C, gsum[0:C, W : 2 * W], jnp.sum(bias_total, axis=1, keepdims=True))

    def piece(k, whole=gsum):
        if isinstance(k, int):
            return whole.at[24 * (k // 2) : 24 * (k // 2) + 24, W * (k % 2) : W * (k % 2) + W]
        return whole.at[pl.ds(pl.multiple_of(lax.div(k, 2) * 24, 8), 24), pl.ds(pl.multiple_of(lax.rem(k, 2) * W, W), W)]

    high, low = lax.div(r, 8), lax.div(c, 4)
    near, far = low * 8 + lax.rem(r, 8), high * 4 + mod4(c)

    def near_id(k):
        return high * 8 + k % 8, k // 8 * 4 + mod4(c)

    def far_id(k):
        return k // 4 * 8 + lax.rem(r, 8), low * 4 + k % 4

    def rs_copy(k, slot):
        return pltpu.make_async_remote_copy(
            piece(k), rs_in.at[slot], rs_ssem.at[k], rs_rsem.at[slot], device_id=near_id(k), device_id_type=MESH)

    def ar_copy(k, slot):
        return pltpu.make_async_remote_copy(
            rs_mine, ar_in.at[slot], ar_ssem.at[k], ar_rsem.at[slot], device_id=far_id(k), device_id_type=MESH)

    def ag_copy(k, slot):
        return pltpu.make_async_remote_copy(
            piece(near, gall), piece(slot, gall), ag_ssem.at[k], ag_rsem.at[slot], device_id=near_id(k), device_id_type=MESH)

    def drain(stops, s, sems):
        for n in range(PIECES // 2):
            for mode in range(2):
                relay_sent(stops, s, (mode, n), sems)

    others(16, near, lambda k: rs_copy(k, near).start())
    ghalo.pack()
    ghalo.start()
    each(range(8), lambda n: pass_on(mstops, 1, n, msems))
    xhalo.sent()
    for s in range(3):
        drain(cstops, s, csems)
    rs_in[near] = piece(near)[...]
    others(16, near, lambda k: rs_copy(k, k).wait_recv())
    rs_mine[...] = jnp.sum(rs_in[...], axis=0)
    others(8, far, lambda k: ar_copy(k, far).start())
    each(range(8, 16), lambda n: pass_on(mstops, 1, n, msems))
    ghalo.columns_in()

    def backward(i):
        row = 4 * i
        back = jnp.dot(wb[:, 0 : 9 * C], tap_rows(gs, row, 4), preferred_element_type=F32)
        for k in range(4):
            flat[pl.ds(row + k, C, stride=R), :] = back[:, k * W : (k + 1) * W]

    loop(8, lambda i: backward(i + 2))
    ar_in[far] = rs_mine[...]
    others(8, far, lambda k: ar_copy(k, k).wait_recv())
    piece(near, gall)[...] = jnp.sum(ar_in[...], axis=0) * (1.0 / 1024)
    others(16, near, lambda k: ag_copy(k, near).start())

    loop(4, lambda i: backward(i + 10))
    ghalo.rows_in()
    for i in (0, 1, 14, 15):
        backward(i)

    def input_out(i):
        for h in range(2):
            ch = i + PIECES * h
            gm = cot_in[ch].astype(F32) + c3[i, h].astype(F32)
            x_in[ch] = (gm + flat[pl.ds(pl.multiple_of(ch * R, R), R), :]).astype(BF16)

    loop(PIECES, input_out, 2)
    gin_copy = pltpu.make_async_copy(x_in, gin_ref, in_sem.at[0])
    gin_copy.start()

    ghalo.sent()
    for s in range(2):
        drain(mstops, s, msems)
    others(16, near, lambda k: rs_copy(k, near).wait_send())
    others(8, far, lambda k: ar_copy(k, far).wait_send())

    def sym_out(n):
        for mode in range(2):
            i = 2 * n + mode
            relay_arrived(mstops, 2, (mode, n), msems)
            for h, flipped in enumerate(unfold(m3, i)):
                ch = i + PIECES * h
                mixed[ch] = (mixed[ch].astype(F32) + flipped).astype(BF16)

    def sym_copy(k, h):
        part = pl.ds(pl.multiple_of(8 * k + PIECES * h, 8), 8)
        return pltpu.make_async_copy(mixed.at[part], sym_ref.at[part], out_sem.at[2 * k + h])

    def sym_part(k):
        loop(4, lambda m: sym_out(4 * k + m))
        sym_copy(k, 0).start()
        sym_copy(k, 1).start()

    loop(4, sym_part)
    drain(mstops, 2, msems)
    others(16, near, lambda k: ag_copy(k, k).wait_recv())
    g_copy = pltpu.make_async_copy(gall, g_ref, in_sem.at[1])
    g_copy.start()
    gin_copy.wait()
    g_copy.wait()
    for k in range(4):
        sym_copy(k, 0).wait()
        sym_copy(k, 1).wait()
    others(16, near, lambda k: ag_copy(k, near).wait_send())


def place_kernel(sym_ref, gin_ref, g_ref, sym_out, gin_out, gw_out, gb_out, sym, gin, grads, gw, came, went):
    g_in = pltpu.make_async_copy(g_ref, grads, came.at[4])
    g_in.start()
    ins, outs = [], []
    for k in range(2):
        part = pl.ds(k * C // 2, C // 2)
        for n, (a, b, room) in enumerate(((sym_ref, sym_out, sym), (gin_ref, gin_out, gin))):
            ins.append(pltpu.make_async_copy(a.at[part], room.at[part], came.at[2 * k + n]))
            outs.append(pltpu.make_async_copy(room.at[part], b.at[part], went.at[2 * k + n]))
    for copy in ins:
        copy.start()
    g_in.wait()
    for p in range(3):
        two = grads[C * p : C * p + C, 0:W]
        gw[p, 0] = two[:, 0:C]
        gw[p, 1] = pltpu.roll(two, C, 1)[:, 0:C]
        gw[p, 2] = grads[C * p : C * p + C, W : W + C]
    gw_copy = pltpu.make_async_copy(gw, gw_out, went.at[4])
    gw_copy.start()
    outs.append(gw_copy)
    gb_out[...] = jnp.transpose(grads[0:C, W : 2 * W], (1, 0))[C : C + 1, :]
    for arrived, copy in zip(ins, outs):
        arrived.wait()
        copy.start()
    for copy in outs:
        copy.wait()


def place(sym, gin, grads):
    hbm = pl.BlockSpec(memory_space=pl.ANY)
    vmem = pl.BlockSpec(memory_space=pltpu.VMEM)
    tile = pltpu.VMEM((C, R, W), BF16)
    return pl.pallas_call(
        place_kernel,
        out_shape=(
            jax.ShapeDtypeStruct((C, R, W), BF16),
            jax.ShapeDtypeStruct((C, R, W), BF16),
            jax.ShapeDtypeStruct((3, 3, C, C), F32),
            jax.ShapeDtypeStruct((1, C), F32),
        ),
        in_specs=[hbm] * 3,
        out_specs=(hbm, hbm, hbm, vmem),
        scratch_shapes=[
            tile, tile, pltpu.VMEM((3 * C, 2 * W), F32), pltpu.VMEM((3, 3, C, C), F32),
            pltpu.SemaphoreType.DMA((5,)), pltpu.SemaphoreType.DMA((5,))],
        compiler_params=pltpu.CompilerParams(vmem_limit_bytes=60 * 1024 * 1024),
    )(sym, gin, grads)


def block(x, weight, bias, cot):
    vmem = pl.BlockSpec(memory_space=pltpu.VMEM)
    hbm = pl.BlockSpec(memory_space=pl.ANY)
    tile = pltpu.VMEM((C, R, W), BF16)
    stop = pltpu.VMEM((PIECES, 2, R, W), BF16)
    stack = pltpu.VMEM((3, R + 4 * D, C, W), BF16)
    pack, edge = pltpu.VMEM((2, 4, C, W), BF16), pltpu.VMEM((2, 6, C, W), BF16)
    weights = pltpu.VMEM((C, 640), BF16)
    dma = pltpu.SemaphoreType.DMA
    sym, gin, grads = pl.pallas_call(
        kernel,
        out_shape=(
            jax.ShapeDtypeStruct((C, R, W), BF16),
            jax.ShapeDtypeStruct((C, R, W), BF16),
            jax.ShapeDtypeStruct((3 * C, 2 * W), F32),
        ),
        in_specs=[hbm, hbm, vmem, vmem],
        out_specs=[hbm] * 3,
        scratch_shapes=[
            tile, tile, weights, weights, pltpu.VMEM((C, W), F32),
            pltpu.VMEM((C * R, W), F32), stack, stack, pltpu.VMEM((R + 4 * D, C, W), BF16),
            pltpu.VMEM((R, C, W), F32), tile, pack, edge, pack, edge,
            stop, stop, stop, stop, stop, stop, stop, stop,
            pltpu.VMEM((3 * C, 2 * W), F32), pltpu.VMEM((3 * C, 2 * W), F32),
            pltpu.VMEM((16, 24, W), F32), pltpu.VMEM((24, W), F32),
            pltpu.VMEM((8, 24, W), F32),
            dma((2,)), dma((8,)), dma((8,)), dma((8,)), dma((8,)), dma((8,)),
            dma((4, PIECES)), dma((4, PIECES)), dma((4, PIECES)), dma((4, PIECES)),
            dma((16,)), dma((16,)), dma((8,)), dma((8,)), dma((16,)), dma((16,)),
        ],
        compiler_params=pltpu.CompilerParams(
            collective_id=0, has_side_effects=True, vmem_limit_bytes=60 * 1024 * 1024),
    )(x, cot, weight, bias.reshape(1, C))
    sym, gin, gw, gb = place(sym, gin, grads)
    return sym, gin, gw, gb.reshape(C)


def solution(mesh):
    tile = P(None, "row", "col")
    return jax.shard_map(
        block,
        mesh=mesh,
        in_specs=(tile, P(), P(), tile),
        out_specs=(tile, tile, P(), P()),
        check_vma=False,
    )
```
